512 devices in a mesh: dp: 8 (over z_hi, core), frames: 4 (over x), rows: 16 (over y, z_lo).
Axes of the slice: x: 4, y: 4, z: 16 (z_hi: 4, z_lo: 4; z = z_hi * 4 + z_lo), core: 2. Of those that a mesh axis runs over, the one named last changes fastest.
Arguments:
- acts_fine: bfloat16 [8, 8, 64, 16, 512], P('dp', 'frames', 'rows'), may hold values from -120 to 120
- acts_coarse: bfloat16 [8, 8, 32, 8, 512], P('dp', 'frames', 'rows'), may hold values from -120 to 120
- grad_coarse: bfloat16 [8, 8, 32, 8, 512], P('dp', 'frames', 'rows'), may hold values from -20 to 20
- gain_fine: float32 [512], replicated, may hold values from 0.5 to 1.5
- bias_fine: float32 [512], replicated, may hold values from -1 to 1
- kernel_fine: bfloat16 [27, 512, 512], P(None, 'rows'), may hold values from -0.0546875 to 0.0546875
- gain_coarse: float32 [512], replicated, may hold values from 0.5 to 1.5
- bias_coarse: float32 [512], replicated, may hold values from -1 to 1
- kernel_coarse: bfloat16 [27, 512, 512], P(None, 'rows'), may hold values from -0.0546875 to 0.0546875
Outputs:
- grad_fine: bfloat16 [8, 8, 64, 16, 512], P('dp', 'frames', 'rows')
- gain_grad_fine: float32 [512], replicated
- bias_grad_fine: float32 [512], replicated
- gain_grad_coarse: float32 [512], replicated
- bias_grad_coarse: float32 [512], replicated
The draws below stay inside these ranges and needn't reach their ends.
All inputs are finite; a program needn't handle non-finite values.
Results may differ from the reference program's by a relative error of at most 0.0048.
Values may be sent and summed in bfloat16 or wider, within the bound.
A program may use at most 64 MiB of HBM per device.

```python
import jax
import jax.numpy as jnp
from jax import lax

C = 512
GROUPS = 32
WIDTH = 16
CLIPS = 8
FRAMES = 8
HEIGHT = 64


def ramped(key, dims_shape, chan_low, chan_high, offset_size):
    key_list = jax.random.split(key, 3)
    clip_count, frame_num, height, col_width, channels = dims_shape
    time_pos = jnp.arange(frame_num, dtype=jnp.float32) / max(frame_num - 1, 1)
    row_pos = jnp.arange(height, dtype=jnp.float32) / max(height - 1, 1)
    ramp_scale = (1.0 + 2.0 * time_pos)[None, :, None, None, None] * (1.0 + 2.0 * row_pos)[None, None, :, None, None]
    scales = jnp.exp(jax.random.uniform(key_list[0], (channels,), jnp.float32, jnp.log(chan_low), jnp.log(chan_high)))
    offsets = offset_size * jax.random.uniform(key_list[1], (channels,), jnp.float32, -1.0, 1.0)
    noise_field = jnp.clip(jax.random.normal(key_list[2], dims_shape, jnp.float32), -4.0, 4.0)
    return offsets * scales + scales * ramp_scale * noise_field


def draw_acts_fine(key, part):
    return ramped(jax.random.fold_in(key, 11), (CLIPS, FRAMES, HEIGHT, WIDTH, C), 0.3, 3.0, 1.0).astype(jnp.bfloat16)


def draw_acts_coarse(key, part):
    return ramped(jax.random.fold_in(key, 12), (CLIPS, FRAMES, HEIGHT // 2, WIDTH // 2, C), 0.3, 3.0, 1.0).astype(jnp.bfloat16)


def draw_grad_coarse(key, part):
    return ramped(jax.random.fold_in(key, 13), (CLIPS, FRAMES, HEIGHT // 2, WIDTH // 2, C), 0.17, 0.5, 0.3).astype(jnp.bfloat16)


def shard_levels(stream_key, dims, shards, least, largest):
    level = 1.0
    for axis_at, blocks in shards:
        draws = jax.random.uniform(jax.random.fold_in(jax.random.fold_in(stream_key, 6), axis_at), (blocks,), jnp.float32, least / len(shards), largest / len(shards))
        level = level * jnp.repeat(jnp.exp(draws), dims[axis_at] // blocks).reshape((-1,) + (1,) * (len(dims) - 1 - axis_at))
    return level


def gaussian(rng, extent, scale, limit, shards=(), kind=jnp.bfloat16):
    values = scale * jax.random.normal(rng, extent, jnp.float32)
    if shards:
        values = values * shard_levels(rng, extent, shards, -0.22, 0.18)
    return jnp.clip(values, -limit, limit).astype(kind)


def setup_inputs(seed: int = 0) -> dict:
    arg_keys = jax.random.split(jax.random.key(seed), 10)
    acts_fine = draw_acts_fine(jax.random.fold_in(arg_keys[9], 71), 0)
    acts_coarse = draw_acts_coarse(jax.random.fold_in(arg_keys[9], 71), 0)
    grad_coarse = draw_grad_coarse(jax.random.fold_in(arg_keys[9], 71), 0)
    gain_fine = jnp.clip(jax.random.uniform(arg_keys[3], (C,), jnp.float32, 0.5, 1.5), 0.5, 1.5)
    bias_fine = jnp.clip(jax.random.uniform(arg_keys[4], (C,), jnp.float32, -1.0, 1.0), -1.0, 1.0)
    kernel_fine = gaussian(arg_keys[5], (27, C, C), (27 * C) ** -0.5, 0.0546875, ((1, 16),))
    gain_coarse = jnp.clip(jax.random.uniform(arg_keys[6], (C,), jnp.float32, 0.5, 1.5), 0.5, 1.5)
    bias_coarse = jnp.clip(jax.random.uniform(arg_keys[7], (C,), jnp.float32, -1.0, 1.0), -1.0, 1.0)
    kernel_coarse = gaussian(arg_keys[8], (27, C, C), (27 * C) ** -0.5, 0.0546875, ((1, 16),))
    return {"acts_fine": acts_fine, "acts_coarse": acts_coarse, "grad_coarse": grad_coarse, "gain_fine": gain_fine, "bias_fine": bias_fine, "kernel_fine": kernel_fine, "gain_coarse": gain_coarse, "bias_coarse": bias_coarse, "kernel_coarse": kernel_coarse}


EPSILON = 1e-06

def transposed_conv(cotangent, kernel):
    frame_num, height, col_width, channels = cotangent.shape
    padded = jnp.pad(cotangent.astype(jnp.float32), ((0, 2), (1, 1), (1, 1), (0, 0)))
    weights = kernel.astype(jnp.float32)
    accumulated = jnp.zeros((frame_num, height, col_width, channels), jnp.float32)
    for tap_index in range(27):
        time_tap = tap_index // 9
        row_tap = tap_index // 3 % 3
        col_tap = tap_index % 3
        window = padded[2 - time_tap:2 - time_tap + frame_num, 2 - row_tap:2 - row_tap + height, 2 - col_tap:2 - col_tap + col_width]
        accumulated = accumulated + jnp.einsum('thwo,io->thwi', window, weights[tap_index])
    return accumulated

def group_back(acts, cotangent, gain, bias, kernel):
    conv_grad = transposed_conv(cotangent, kernel)
    values = acts.astype(jnp.float32)
    frame_num, height, col_width, channels = values.shape
    group_width = channels // GROUPS
    entries = frame_num * height * col_width * group_width
    grouped = values.reshape(-1, GROUPS, group_width)
    group_mean = lax.optimization_barrier(jnp.sum(grouped, axis=(0, 2))) / entries
    square = lax.optimization_barrier(jnp.sum(grouped * grouped, axis=(0, 2))) / entries
    inv_std = lax.rsqrt(square - group_mean * group_mean + EPSILON)
    mean_chan = jnp.repeat(group_mean, group_width)
    inv_chan = jnp.repeat(inv_std, group_width)
    normed = (values - mean_chan) * inv_chan
    preact = gain * normed + bias
    squash = jax.nn.sigmoid(preact)
    pre_grad = conv_grad * squash * (1.0 + preact * (1.0 - squash))
    sum_one = lax.optimization_barrier(jnp.sum(pre_grad, axis=(0, 1, 2)))
    sum_two = lax.optimization_barrier(jnp.sum(pre_grad * normed, axis=(0, 1, 2)))
    group_one = lax.optimization_barrier(jnp.sum((gain * sum_one).reshape(GROUPS, group_width), axis=1)) / entries
    group_two = lax.optimization_barrier(jnp.sum((gain * sum_two).reshape(GROUPS, group_width), axis=1)) / entries
    level_grad = cotangent.astype(jnp.float32) + inv_chan * (gain * pre_grad - jnp.repeat(group_one, group_width) - normed * jnp.repeat(group_two, group_width))
    return (level_grad, sum_one, sum_two)

def reference(acts_fine, acts_coarse, grad_coarse, gain_fine, bias_fine, kernel_fine, gain_coarse, bias_coarse, kernel_coarse):

    def per_clip(clip_items):
        fine_acts, coarse_acts, cotangent = clip_items
        coarse_input_grad, coarse_one, coarse_two = group_back(coarse_acts, cotangent, gain_coarse, bias_coarse, kernel_coarse)
        upsampled = (jnp.repeat(jnp.repeat(coarse_input_grad, 2, axis=1), 2, axis=2) * 0.25).astype(jnp.bfloat16)
        fine_grad, fine_one, fine_two = group_back(fine_acts, upsampled, gain_fine, bias_fine, kernel_fine)
        return (fine_grad.astype(jnp.bfloat16), fine_one, fine_two, coarse_one, coarse_two)
    results = lax.map(per_clip, (acts_fine, acts_coarse, grad_coarse))
    scale_fine = 1.0 / jnp.sqrt(jnp.float32(CLIPS * FRAMES * HEIGHT * WIDTH))
    scale_coarse = 1.0 / jnp.sqrt(jnp.float32(CLIPS * FRAMES * HEIGHT * WIDTH // 4))
    gain_grad_fine = lax.optimization_barrier(jnp.sum(results[2], axis=0)) * scale_fine
    bias_grad_fine = lax.optimization_barrier(jnp.sum(results[1], axis=0)) * scale_fine
    gain_grad_coarse = lax.optimization_barrier(jnp.sum(results[4], axis=0)) * scale_coarse
    bias_grad_coarse = lax.optimization_barrier(jnp.sum(results[3], axis=0)) * scale_coarse
    return (results[0], gain_grad_fine, bias_grad_fine, gain_grad_coarse, bias_grad_coarse)
```

```python
import functools

import jax
import jax.numpy as jnp
from jax import lax
from jax.experimental import pallas as pl
from jax.experimental.pallas import tpu as pltpu
from jax.sharding import PartitionSpec as P

GROUPS = 32
EPSILON = 1e-06
MESH = pl.DeviceIdType.MESH
LANES = 128


def iota(shape, dim):
    return lax.broadcasted_iota(jnp.int32, shape, dim)


def one_hot(cond, dtype=jnp.bfloat16):
    return jnp.where(cond, 1.0, 0.0).astype(dtype)


def fine_position(new):
    frame, p, q, a, b = new >> 6, (new >> 5) & 1, (new >> 4) & 1, (new >> 3) & 1, new & 7
    return frame * 64 + (2 * a + p) * 16 + 2 * b + q


def chunk_swap(arrays, chunk):
    arrays = list(arrays)
    for bit in range(3):
        step = 1 << bit
        low = ((chunk >> bit) & 1) == 0
        for i in range(8):
            if i & step:
                continue
            one, two = arrays[i], arrays[i + step]
            arrays[i] = jnp.where(low, one, pltpu.roll(two, 16 * step, 1))
            arrays[i + step] = jnp.where(low, pltpu.roll(one, LANES - 16 * step, 1), two)
    return arrays


def group_total(column):
    per_group = column.shape[0] // 2
    split = column.reshape(2, per_group, 1)
    return jnp.broadcast_to(jnp.sum(split, axis=1, keepdims=True), split.shape).reshape(column.shape)


def columns_of(parts, lane):
    block = jnp.zeros(lane.shape, jnp.float32)
    for k, part in enumerate(parts):
        block = jnp.where(lane == k, part, block)
    return block


def row_sum(x):
    return jnp.sum(x, axis=1, keepdims=True)


def kernel(
    sizes,
    acts_fine,
    acts_coarse,
    grad_coarse,
    gain_fine,
    bias_fine,
    gain_coarse,
    bias_coarse,
    kernel_fine,
    kernel_coarse,
    out,
    par,
    weights_f,
    weights_c,
    sent_f,
    sent_c,
    got_f,
    got_c,
    cot,
    quart,
    prod,
    halo_out_c,
    halo_in_c,
    halo_out_f,
    halo_in_f,
    stats,
    par_dp,
    par_rows,
    grad_out,
    grad_in,
    load_sem,
    send_rows,
    recv_rows,
    send_frames,
    recv_frames,
    send_halo,
    recv_halo,
    send_dp,
    recv_dp,
):
    n_dp, n_frames, n_rows = sizes
    dp, fr, row = lax.axis_index("dp"), lax.axis_index("frames"), lax.axis_index("rows")
    width = weights_f.shape[0] // 27

    loads = [
        pltpu.make_async_copy(kernel_coarse, weights_c, load_sem.at[0]),
        pltpu.make_async_copy(kernel_fine, weights_f, load_sem.at[1]),
    ]
    for load in loads:
        load.start()

    barrier = pltpu.get_barrier_semaphore()
    for axis, me, count in (("rows", row, n_rows), ("frames", fr, n_frames), ("dp", dp, n_dp)):

        def greet(d, carry, axis=axis, me=me, count=count):
            pl.semaphore_signal(barrier, inc=1, device_id={axis: lax.rem(me + d, count)}, device_id_type=MESH)
            return carry

        if count > 1:
            lax.fori_loop(1, count, greet, 0)

    new, old = iota((LANES, LANES), 0), iota((LANES, LANES), 1)
    to_new = one_hot(old == fine_position(new))
    to_old = one_hot(new == fine_position(old))
    moved = jnp.dot(to_new, acts_fine[...], preferred_element_type=jnp.float32)
    sent_f[...] = moved.T.astype(jnp.bfloat16)
    place, source = iota((LANES, 32), 0), iota((LANES, 32), 1)
    eighth = lax.rem(row, 8)
    at_first = ((place >> 4) == eighth) & (source == (place & 15))
    at_second = ((place >> 4) == lax.rem(eighth + 4, 8)) & (source == 16 + (place & 15))
    placed = jnp.dot(one_hot(at_first | at_second), acts_coarse[...], preferred_element_type=jnp.float32)
    sent_c[...] = placed.T.astype(jnp.bfloat16)

    pl.semaphore_wait(barrier, (n_rows - 1) + (n_frames - 1) + (n_dp - 1))

    def slices(ref, index):
        return ref.at[pl.ds(pl.multiple_of(index * width, width), width)]

    def rows_copy(stage, target, source):
        if stage == 0:
            src, dst = grad_coarse, cot.at[:, source]
        elif stage == 1:
            src, dst = slices(sent_c, target), got_c.at[source]
        elif stage == 2:
            src, dst = slices(sent_f, target), got_f.at[source]
        elif stage == 3:
            src, dst = quart.at[row], quart.at[source]
        elif stage == 4:
            src, dst = grad_out.at[target], grad_in.at[source]
        else:
            src, dst = par_rows.at[row], par_rows.at[source]
        return pltpu.make_async_remote_copy(
            src_ref=src,
            dst_ref=dst,
            send_sem=send_rows.at[stage, target],
            recv_sem=recv_rows.at[stage, source],
            device_id={"rows": target},
            device_id_type=MESH,
        )

    def rows_send(stage):
        def step(d, carry):
            rows_copy(stage, lax.rem(row + d, n_rows), row).start()
            return carry

        lax.fori_loop(1, n_rows, step, 0)

    def rows_wait(stage):
        def step(d, carry):
            other = lax.rem(row + n_rows - d, n_rows)
            rows_copy(stage, other, other).wait_recv()
            return carry

        lax.fori_loop(1, n_rows, step, 0)

    def rows_sent(stage):
        def step(d, carry):
            rows_copy(stage, lax.rem(row + d, n_rows), row).wait_send()
            return carry

        lax.fori_loop(1, n_rows, step, 0)

    def frames_copy(stage, target, source):
        return pltpu.make_async_remote_copy(
            src_ref=stats.at[stage, fr],
            dst_ref=stats.at[stage, source],
            send_sem=send_frames.at[stage, target],
            recv_sem=recv_frames.at[stage, source],
            device_id={"frames": target},
            device_id_type=MESH,
        )

    def frames_start(stage, block):
        stats[stage, fr] = block

        def step(d, carry):
            frames_copy(stage, lax.rem(fr + d, n_frames), fr).start()
            return carry

        lax.fori_loop(1, n_frames, step, 0)

    def frames_total(stage):
        def step(d, carry):
            other = lax.rem(fr + n_frames - d, n_frames)
            frames_copy(stage, other, other).wait_recv()
            return carry

        lax.fori_loop(1, n_frames, step, 0)
        total = stats[stage, 0]
        for k in range(1, n_frames):
            total = total + stats[stage, k]
        return total

    def halo_copy(stage):
        src, dst = ((halo_out_c, halo_in_c), (halo_out_f, halo_in_f))[stage]
        return pltpu.make_async_remote_copy(
            src_ref=src,
            dst_ref=dst,
            send_sem=send_halo.at[stage],
            recv_sem=recv_halo.at[stage],
            device_id={"frames": lax.rem(fr + n_frames - 1, n_frames)},
            device_id_type=MESH,
        )

    def halo_send(stage):
        @pl.when(fr > 0)
        def _():
            halo_copy(stage).start()

    def halo_wait(stage):
        @pl.when(fr < n_frames - 1)
        def _():
            halo_copy(stage).wait_recv()

        @pl.when(fr == n_frames - 1)
        def _():
            into = (halo_in_c, halo_in_f)[stage]
            into[...] = jnp.zeros_like(into)

    own = pltpu.make_async_copy(grad_coarse, cot.at[:, row], load_sem.at[2])
    own.start()
    rows_send(0)
    rows_send(1)
    rows_send(2)
    got_c[row] = sent_c[pl.ds(pl.multiple_of(row * width, width), width), :]
    got_f[row] = sent_f[pl.ds(pl.multiple_of(row * width, width), width), :]

    wide = iota((width, gain_fine.shape[1]), 1) == row * width + iota((width, gain_fine.shape[1]), 0)

    def column(vector):
        return row_sum(jnp.where(wide, vector[...], 0.0))

    gain_f, bias_f, gain_c, bias_c = (column(v) for v in (gain_fine, bias_fine, gain_coarse, bias_coarse))
    lane = iota((width, LANES), 1)
    chunk = lane >> 4

    cells = 256
    spot = iota((width, cells), 1)
    top, bottom = spot >= 8, spot < cells - 8
    left, right = (spot & 7) > 0, (spot & 7) < 7

    def above(x):
        return jnp.where(top, pltpu.roll(x, 8, 1), 0.0)

    def below(x):
        return jnp.where(bottom, pltpu.roll(x, cells - 8, 1), 0.0)

    def before(x):
        return jnp.where(left, pltpu.roll(x, 1, 1), 0.0)

    def after(x):
        return jnp.where(right, pltpu.roll(x, cells - 1, 1), 0.0)

    def product(depth, tap, frame):
        at = (depth * 9 + tap) * width
        return prod[at : at + width, frame * cells : (frame + 1) * cells]

    def spatial_taps(which):
        terms = (((0, 0),), ((1, 0), (0, 1)), ((2, 0), (1, 1)), ((2, 1),))[which]
        taps = []
        for tap in range(9):
            total = product(terms[0][0], tap, terms[0][1])
            for depth, frame in terms[1:]:
                total = total + product(depth, tap, frame)
            taps.append(total)
        return taps

    def coarse_frame(which):
        t = spatial_taps(which)
        r = [below(t[kw]) + t[3 + kw] + above(t[6 + kw]) for kw in range(3)]
        return after(r[0]) + r[1] + before(r[2])

    def fine_frame(which):
        t = spatial_taps(which)
        planes = []
        for p in range(2):
            if p == 0:
                r = [t[kw] + t[3 + kw] + above(t[6 + kw]) for kw in range(3)]
            else:
                r = [below(t[kw]) + t[3 + kw] + t[6 + kw] for kw in range(3)]
            planes.append(r[0] + r[1] + before(r[2]))
            planes.append(after(r[0]) + r[1] + r[2])
        return planes

    rows_wait(1)
    firsts, seconds = [], []
    for half in range(2):
        first = jnp.zeros((width, LANES), jnp.float32)
        second = jnp.zeros((width, LANES), jnp.float32)
        for j in range(8):
            block = got_c[8 * half + j].astype(jnp.float32)
            first = jnp.where(chunk == j, block, first)
            second = jnp.where(chunk == (j + 4) % 8, block, second)
        firsts.append(first)
        seconds.append(pltpu.roll(second, 64, 1))
    values_c = jnp.concatenate(firsts + seconds, axis=1)
    rows_wait(2)
    swapped = []
    for half in range(2):
        swapped.append(chunk_swap([got_f[8 * half + j].astype(jnp.float32) for j in range(8)], chunk))
    values_f = jnp.concatenate([swapped[half][c] for c in range(8) for half in range(2)], axis=1)
    frames_start(
        0,
        columns_of(
            (row_sum(values_f), row_sum(values_f * values_f), row_sum(values_c), row_sum(values_c * values_c)), lane
        ),
    )

    loads[0].wait()
    own.wait()
    rows_wait(0)
    gathered = cot[...].reshape(2 * n_rows * 16, cot.shape[3])
    nt = (((1,), (1,)), ((), ()))
    prod[...] = lax.dot_general(weights_c[...], gathered, nt, preferred_element_type=jnp.float32)
    halo_out_c[:, 0:cells] = coarse_frame(0)
    halo_out_c[:, cells:] = coarse_frame(1)
    halo_send(0)
    conv_c = jnp.concatenate([coarse_frame(2), coarse_frame(3)], axis=1)
    picked = one_hot(wide)
    cot_c = lax.dot_general(picked, gathered, nt, preferred_element_type=jnp.float32)

    entries_c = 16 * 2 * n_frames * cells
    entries_f = 4 * entries_c
    moments = frames_total(0)

    def norm_of(at, entries):
        mean = group_total(moments[:, at : at + 1]) / entries
        square = group_total(moments[:, at + 1 : at + 2]) / entries
        return mean, lax.rsqrt(square - mean * mean + EPSILON)

    def through(values, gain, bias, mean, inv):
        normed = (values - mean) * inv
        pre = gain * normed + bias
        squash = jax.nn.sigmoid(pre)
        return normed, squash * (1.0 + pre * (1.0 - squash))

    mean_c, inv_c = norm_of(2, entries_c)
    mean_f, inv_f = norm_of(0, entries_f)
    normed_c, slope_c = through(values_c, gain_c, bias_c, mean_c, inv_c)

    halo_wait(0)
    pre_grad_c = (conv_c + halo_in_c[...]) * slope_c
    frames_start(1, columns_of((row_sum(pre_grad_c), row_sum(pre_grad_c * normed_c)), lane))
    totals_c = frames_total(1)
    one_c, two_c = totals_c[:, 0:1], totals_c[:, 1:2]

    def level(cot, normed, pre_grad, gain, inv, one, two, entries):
        group_one = group_total(gain * one) / entries
        group_two = group_total(gain * two) / entries
        return cot + inv * (gain * pre_grad - group_one - normed * group_two)

    level_c = level(cot_c, normed_c, pre_grad_c, gain_c, inv_c, one_c, two_c, entries_c)
    quarter = (level_c * 0.25).astype(jnp.bfloat16)
    quart[row] = quarter
    rows_send(3)

    normed_f, slope_f = through(values_f, gain_f, bias_f, mean_f, inv_f)
    loads[1].wait()
    rows_wait(3)
    prod[...] = jnp.dot(
        weights_f[...], quart[...].reshape(n_rows * width, 2 * cells), preferred_element_type=jnp.float32
    )
    for which in range(2):
        halo_out_f[:, which * 4 * cells : (which + 1) * 4 * cells] = jnp.concatenate(
            fine_frame(which), axis=1
        ).astype(halo_out_f.dtype)
    halo_send(1)
    conv_f = jnp.concatenate(fine_frame(2) + fine_frame(3), axis=1)
    halo_wait(1)
    pre_grad_f = (conv_f + halo_in_f[...].astype(jnp.float32)) * slope_f
    frames_start(2, columns_of((row_sum(pre_grad_f), row_sum(pre_grad_f * normed_f)), lane))
    totals_f = frames_total(2)
    one_f, two_f = totals_f[:, 0:1], totals_f[:, 1:2]

    spread = lane == lax.rem(row, 4) * width + iota((width, LANES), 0)
    which_row = iota((8, LANES), 0)
    mine = jnp.zeros((8, LANES), jnp.float32)
    cells_all = n_dp * 2 * n_frames * cells
    scale_c, scale_f = 1.0 / cells_all**0.5, 1.0 / (4 * cells_all) ** 0.5
    for k, (sums, scale) in enumerate(((two_f, scale_f), (one_f, scale_f), (two_c, scale_c), (one_c, scale_c))):
        line = jnp.sum(jnp.where(spread, sums, 0.0), axis=0, keepdims=True) * scale
        mine = jnp.where(which_row == k, line, mine)
    par_dp[dp] = mine

    def dp_copy(target, source):
        return pltpu.make_async_remote_copy(
            src_ref=par_dp.at[dp],
            dst_ref=par_dp.at[source],
            send_sem=send_dp.at[target],
            recv_sem=recv_dp.at[source],
            device_id={"dp": target},
            device_id_type=MESH,
        )

    def dp_start(d, carry):
        dp_copy(lax.rem(dp + d, n_dp), dp).start()
        return carry

    def dp_wait(d, carry):
        other = lax.rem(dp + n_dp - d, n_dp)
        dp_copy(other, other).wait_recv()
        return carry

    def dp_sent(d, carry):
        dp_copy(lax.rem(dp + d, n_dp), dp).wait_send()
        return carry

    if n_dp > 1:
        lax.fori_loop(1, n_dp, dp_start, 0)

    four = [quarter[:, frame * cells : (frame + 1) * cells].astype(jnp.float32) for frame in range(2)]
    cot_f = jnp.concatenate([four[c // 4] for c in range(8)], axis=1)
    level_f = level(cot_f, normed_f, pre_grad_f, gain_f, inv_f, one_f, two_f, entries_f)
    for half in range(2):
        planes = [level_f[:, c * cells + half * LANES : c * cells + (half + 1) * LANES] for c in range(8)]
        for j, block in enumerate(chunk_swap(planes, chunk)):
            grad_out[8 * half + j] = block.astype(jnp.bfloat16)
    rows_send(4)
    grad_in[row] = grad_out[row]

    if n_dp > 1:
        lax.fori_loop(1, n_dp, dp_wait, 0)
    total = par_dp[0]
    for k in range(1, n_dp):
        total = total + par_dp[k]
    par_rows[row] = total
    rows_send(5)

    rows_wait(4)
    back = grad_in[...].reshape(n_rows * width, LANES).astype(jnp.float32).T.astype(jnp.bfloat16)
    out[...] = jnp.dot(to_old, back, preferred_element_type=jnp.float32).astype(out.dtype)

    rows_wait(5)
    for c in range(par.shape[1] // LANES):
        total = par_rows[4 * c]
        for k in range(1, 4):
            total = total + par_rows[4 * c + k]
        par[:, c * LANES : (c + 1) * LANES] = total

    for stage in range(6):
        rows_sent(stage)
    for stage in range(3):

        def frames_sent(d, carry, stage=stage):
            frames_copy(stage, lax.rem(fr + d, n_frames), fr).wait_send()
            return carry

        lax.fori_loop(1, n_frames, frames_sent, 0)

    @pl.when(fr > 0)
    def _():
        halo_copy(0).wait_send()
        halo_copy(1).wait_send()

    if n_dp > 1:
        lax.fori_loop(1, n_dp, dp_sent, 0)


def shards(
    sizes,
    acts_fine,
    acts_coarse,
    grad_coarse,
    gain_fine,
    bias_fine,
    kernel_fine,
    gain_coarse,
    bias_coarse,
    kernel_coarse,
):
    n_dp, n_frames, n_rows = sizes
    channels = acts_fine.shape[-1]
    width = channels // n_rows
    positions = 2 * n_rows * 16
    bf16, f32 = jnp.bfloat16, jnp.float32
    vmem = pl.BlockSpec(memory_space=pltpu.VMEM)
    anywhere = pl.BlockSpec(memory_space=pl.ANY)
    dma = pltpu.SemaphoreType.DMA
    taps = kernel_fine.shape[0]
    out, par = pl.pallas_call(
        functools.partial(kernel, sizes),
        out_shape=(
            jax.ShapeDtypeStruct((LANES, channels), bf16),
            jax.ShapeDtypeStruct((8, channels), f32),
        ),
        in_specs=[vmem] * 7 + [anywhere] * 2,
        out_specs=(vmem, vmem),
        scratch_shapes=[
            pltpu.VMEM((taps * width, channels), bf16),
            pltpu.VMEM((taps * width, channels), bf16),
            pltpu.VMEM((channels, LANES), bf16),
            pltpu.VMEM((channels, LANES), bf16),
            pltpu.VMEM((n_rows, width, LANES), bf16),
            pltpu.VMEM((n_rows, width, LANES), bf16),
            pltpu.VMEM((2, n_rows, 16, channels), bf16),
            pltpu.VMEM((n_rows, width, positions), bf16),
            pltpu.VMEM((taps * width, positions), f32),
            pltpu.VMEM((width, positions), f32),
            pltpu.VMEM((width, positions), f32),
            pltpu.VMEM((width, 4 * positions), bf16),
            pltpu.VMEM((width, 4 * positions), bf16),
            pltpu.VMEM((3, n_frames, width, LANES), f32),
            pltpu.VMEM((n_dp, 8, LANES), f32),
            pltpu.VMEM((n_rows, 8, LANES), f32),
            pltpu.VMEM((n_rows, width, LANES), bf16),
            pltpu.VMEM((n_rows, width, LANES), bf16),
            dma((3,)),
            dma((6, n_rows)),
            dma((6, n_rows)),
            dma((3, n_frames)),
            dma((3, n_frames)),
            dma((2,)),
            dma((2,)),
            dma((n_dp,)),
            dma((n_dp,)),
        ],
        compiler_params=pltpu.CompilerParams(collective_id=0, has_side_effects=True),
        name="levels",
    )(
        acts_fine.reshape(LANES, channels),
        acts_coarse.reshape(32, channels),
        grad_coarse.reshape(2, 16, channels),
        gain_fine.reshape(1, channels),
        bias_fine.reshape(1, channels),
        gain_coarse.reshape(1, channels),
        bias_coarse.reshape(1, channels),
        kernel_fine.reshape(taps * width, channels),
        kernel_coarse.reshape(taps * width, channels),
    )
    return (out.reshape(acts_fine.shape), par[0], par[1], par[2], par[3])


def solution(mesh):
    sizes = (mesh.shape["dp"], mesh.shape["frames"], mesh.shape["rows"])
    tall = P("dp", "frames", "rows", None, None)
    in_specs = (tall, tall, tall, P(), P(), P(None, "rows", None), P(), P(), P(None, "rows", None))
    out_specs = (tall, P(), P(), P(), P())
    return jax.shard_map(
        functools.partial(shards, sizes), mesh=mesh, in_specs=in_specs, out_specs=out_specs, check_vma=False
    )
```

```python
import functools

import jax
import jax.numpy as jnp
from jax import lax
from jax.experimental import pallas as pl
from jax.experimental.pallas import tpu as pltpu
from jax.sharding import PartitionSpec as P

GROUPS = 32
EPSILON = 1e-06
MESH = pl.DeviceIdType.MESH
LANES = 128


def iota(shape, dim):
    return lax.broadcasted_iota(jnp.int32, shape, dim)


def one_hot(cond, dtype=jnp.bfloat16):
    return jnp.where(cond, 1.0, 0.0).astype(dtype)


def fine_position(new):
    frame, p, q, a, b = new >> 6, (new >> 5) & 1, (new >> 4) & 1, (new >> 3) & 1, new & 7
    return frame * 64 + (2 * a + p) * 16 + 2 * b + q


def chunk_swap(arrays, chunk):
    arrays = list(arrays)
    for bit in range(3):
        step = 1 << bit
        low = ((chunk >> bit) & 1) == 0
        for i in range(8):
            if i & step:
                continue
            one, two = arrays[i], arrays[i + step]
            arrays[i] = jnp.where(low, one, pltpu.roll(two, 16 * step, 1))
            arrays[i + step] = jnp.where(low, pltpu.roll(one, LANES - 16 * step, 1), two)
    return arrays


def group_total(column):
    per_group = column.shape[0] // 2
    split = column.reshape(2, per_group, 1)
    return jnp.broadcast_to(jnp.sum(split, axis=1, keepdims=True), split.shape).reshape(column.shape)


def row_of(columns, diagonal):
    spread = jnp.zeros(diagonal.shape, jnp.float32)
    for k, column in enumerate(columns):
        spread = jnp.where(diagonal == k, column, spread)
    return jnp.sum(spread, axis=0, keepdims=True)


def column_of(row, diagonal, k):
    return row_sum(jnp.where(diagonal == k, row, 0.0))


def row_sum(x):
    return jnp.sum(x, axis=1, keepdims=True)


def kernel(
    sizes,
    acts_fine,
    acts_coarse,
    grad_coarse,
    gain_fine,
    bias_fine,
    gain_coarse,
    bias_coarse,
    kernel_fine,
    kernel_coarse,
    out,
    par,
    weights_f,
    weights_c,
    sent_f,
    sent_c,
    got_f,
    got_c,
    cot,
    quart,
    prod,
    halo_out_c,
    halo_in_c,
    halo_out_f,
    halo_in_f,
    stats,
    par_dp,
    par_rows,
    grad_out,
    grad_in,
    load_sem,
    send_rows,
    recv_rows,
    send_frames,
    recv_frames,
    send_halo,
    recv_halo,
    send_dp,
    recv_dp,
    send_relay,
    recv_relay,
    ready,
):
    n_dp, n_frames, n_rows = sizes
    dp, fr, row = lax.axis_index("dp"), lax.axis_index("frames"), lax.axis_index("rows")
    width = weights_f.shape[0] // 27

    loads = [
        pltpu.make_async_copy(kernel_coarse, weights_c, load_sem.at[0]),
        pltpu.make_async_copy(kernel_fine, weights_f, load_sem.at[1]),
    ]
    for load in loads:
        load.start()

    even = dp + 1 - 2 * lax.rem(dp, 2)
    ring = [lax.rem(dp + step, n_dp) for step in (2, n_dp - 2)] if n_dp == 8 else []
    near_dp = [even] + ring + [lax.rem(even + step, n_dp) for step in (2, n_dp - 2)] if n_dp == 8 else []
    barrier = pltpu.get_barrier_semaphore()
    for axis, me, count in (("rows", row, n_rows), ("frames", fr, n_frames)):

        def greet(d, carry, axis=axis, me=me, count=count):
            pl.semaphore_signal(barrier, inc=1, device_id={axis: lax.rem(me + d, count)}, device_id_type=MESH)
            return carry

        lax.fori_loop(1, count, greet, 0)
    for peer in near_dp:
        pl.semaphore_signal(barrier, inc=1, device_id={"dp": peer}, device_id_type=MESH)

    cot[:, row] = grad_coarse[...]

    new, old = iota((LANES, LANES), 0), iota((LANES, LANES), 1)
    to_new = one_hot(old == fine_position(new))
    to_old = one_hot(new == fine_position(old))
    moved = jnp.dot(to_new, acts_fine[...], preferred_element_type=jnp.float32)
    sent_f[...] = moved.T.astype(jnp.bfloat16)
    place, source = iota((LANES, 32), 0), iota((LANES, 32), 1)
    placed = jnp.dot(one_hot((place & 31) == source), acts_coarse[...], preferred_element_type=jnp.float32)
    quads = placed.T.reshape(n_rows, 4, 8, LANES)
    quad = iota((n_rows, 8, LANES), 2) >> 5
    folded = jnp.where(quad == 0, quads[:, 0], 0.0)
    for k in range(1, 4):
        folded = jnp.where(quad == k, quads[:, k], folded)
    sent_c[...] = folded.astype(jnp.bfloat16)

    pl.semaphore_wait(barrier, (n_rows - 1) + (n_frames - 1) + len(near_dp))
    for peer in ring:
        pl.semaphore_signal(ready, inc=1, device_id={"dp": peer}, device_id_type=MESH)

    def slices(ref, index):
        return ref.at[pl.ds(pl.multiple_of(index * width, width), width)]

    def rows_copy(stage, target, source):
        if stage == 0:
            src, dst = sent_c.at[target], got_c.at[source]
        elif stage == 1:
            src, dst = slices(sent_f, target), got_f.at[source]
        elif stage == 2:
            src, dst = grad_out.at[target], grad_in.at[source]
        else:
            src, dst = par_rows.at[row], par_rows.at[source]
        return pltpu.make_async_remote_copy(
            src_ref=src,
            dst_ref=dst,
            send_sem=send_rows.at[stage, target],
            recv_sem=recv_rows.at[stage, source],
            device_id={"rows": target},
            device_id_type=MESH,
        )

    y, z = lax.div(row, 4), lax.rem(row, 4)
    z_mate = (z, z + 1 - 2 * lax.rem(z, 2), lax.rem(z + 2, 4), 3 - z)
    y_up, y_down, y_far = lax.rem(y + 1, 4), lax.rem(y + 3, 4), lax.rem(y + 2, 4)

    def at(y_of, z_of):
        return 4 * y_of + z_of

    def relay(stage, k, slot, target):
        block = (cot.at[:, slot], quart.at[slot])[stage]
        return pltpu.make_async_remote_copy(
            src_ref=block,
            dst_ref=block,
            send_sem=send_relay.at[stage, k],
            recv_sem=recv_relay.at[stage, slot],
            device_id={"rows": target},
            device_id_type=MESH,
        )

    up, down = at(y_up, z), at(y_down, z)

    def routes():
        own = (None, row, [at(y, z_mate[1]), up, down, at(y, z_mate[2]), at(y, z_mate[3])])
        return [
            own,
            (0, at(y, z_mate[1]), [up, down]),
            (0, at(y_down, z_mate[0]), [up]),
            (0, at(y, z_mate[2]), [up, down]),
            (0, at(y_up, z_mate[1]), [down]),
            (0, at(y, z_mate[3]), [up, down]),
            (0, at(y_down, z_mate[2]), [up]),
            (0, at(y_up, z_mate[3]), [down]),
            (0, at(y_down, z_mate[1]), []),
            (0, at(y_down, z_mate[3]), []),
            (0, at(y_up, z_mate[0]), []),
            (0, at(y_up, z_mate[2]), []),
            (0, at(y_far, z_mate[0]), []),
            (0, at(y_far, z_mate[1]), []),
            (0, at(y_far, z_mate[2]), []),
            (0, at(y_far, z_mate[3]), []),
        ]

    def gather_start(stage):
        for k, target in enumerate(routes()[0][2]):
            relay(stage, k, row, target).start()

    def gather_finish(stage):
        k = 5
        for _, slot, targets in routes()[1:]:
            relay(stage, 0, slot, row).wait_recv()
            for target in targets:
                relay(stage, k, slot, target).start()
                k += 1

    def gather_sent(stage):
        for k in range(15):
            relay(stage, k, row, up).wait_send()

    def rows_send(stage):
        def step(d, carry):
            rows_copy(stage, lax.rem(row + d, n_rows), row).start()
            return carry

        lax.fori_loop(1, n_rows, step, 0)

    def rows_wait(stage):
        def step(d, carry):
            other = lax.rem(row + n_rows - d, n_rows)
            rows_copy(stage, other, other).wait_recv()
            return carry

        lax.fori_loop(1, n_rows, step, 0)

    def rows_sent(stage):
        def step(d, carry):
            rows_copy(stage, lax.rem(row + d, n_rows), row).wait_send()
            return carry

        lax.fori_loop(1, n_rows, step, 0)

    def frames_copy(stage, target, source):
        return pltpu.make_async_remote_copy(
            src_ref=stats.at[stage, fr],
            dst_ref=stats.at[stage, source],
            send_sem=send_frames.at[stage, target],
            recv_sem=recv_frames.at[stage, source],
            device_id={"frames": target},
            device_id_type=MESH,
        )

    def frames_start(stage, block):
        stats[stage, fr] = block

        def step(d, carry):
            frames_copy(stage, lax.rem(fr + d, n_frames), fr).start()
            return carry

        lax.fori_loop(1, n_frames, step, 0)

    def frames_total(stage):
        def step(d, carry):
            other = lax.rem(fr + n_frames - d, n_frames)
            frames_copy(stage, other, other).wait_recv()
            return carry

        lax.fori_loop(1, n_frames, step, 0)
        total = stats[stage, 0]
        for k in range(1, n_frames):
            total = total + stats[stage, k]
        return total

    def halo_copy(stage):
        src, dst = ((halo_out_c, halo_in_c), (halo_out_f, halo_in_f))[stage]
        return pltpu.make_async_remote_copy(
            src_ref=src,
            dst_ref=dst,
            send_sem=send_halo.at[stage],
            recv_sem=recv_halo.at[stage],
            device_id={"frames": lax.rem(fr + n_frames - 1, n_frames)},
            device_id_type=MESH,
        )

    def halo_send(stage):
        @pl.when(fr > 0)
        def _():
            halo_copy(stage).start()

    def halo_wait(stage):
        @pl.when(fr < n_frames - 1)
        def _():
            halo_copy(stage).wait_recv()

        @pl.when(fr == n_frames - 1)
        def _():
            into = (halo_in_c, halo_in_f)[stage]
            into[...] = jnp.zeros_like(into)

    gather_start(0)
    rows_send(0)
    got_c[row] = sent_c[row]

    wide = iota((width, gain_fine.shape[1]), 1) == row * width + iota((width, gain_fine.shape[1]), 0)

    def column(vector):
        return row_sum(jnp.where(wide, vector[...], 0.0))

    gain_f, bias_f, gain_c, bias_c = (column(v) for v in (gain_fine, bias_fine, gain_coarse, bias_coarse))
    lane, channel = iota((width, LANES), 1), iota((width, LANES), 0)
    chunk = lane >> 4
    diagonal = jnp.where((lane & 31) == channel, lane >> 5, -1)

    cells = 256
    spot = iota((width, cells), 1)
    top, bottom = spot >= 8, spot < cells - 8
    left, right = (spot & 7) > 0, (spot & 7) < 7

    def above(x):
        return jnp.where(top, pltpu.roll(x, 8, 1), 0.0)

    def below(x):
        return jnp.where(bottom, pltpu.roll(x, cells - 8, 1), 0.0)

    def before(x):
        return jnp.where(left, pltpu.roll(x, 1, 1), 0.0)

    def after(x):
        return jnp.where(right, pltpu.roll(x, cells - 1, 1), 0.0)

    def product(depth, tap, frame):
        at = (depth * 9 + tap) * width
        return prod[at : at + width, frame * cells : (frame + 1) * cells]

    def spatial_taps(which):
        terms = (((0, 0),), ((1, 0), (0, 1)), ((2, 0), (1, 1)), ((2, 1),))[which]
        taps = []
        for tap in range(9):
            total = product(terms[0][0], tap, terms[0][1])
            for depth, frame in terms[1:]:
                total = total + product(depth, tap, frame)
            taps.append(total)
        return taps

    def coarse_frame(which):
        t = spatial_taps(which)
        r = [below(t[kw]) + t[3 + kw] + above(t[6 + kw]) for kw in range(3)]
        return after(r[0]) + r[1] + before(r[2])

    def fine_frame(which):
        t = spatial_taps(which)
        planes = []
        for p in range(2):
            if p == 0:
                r = [t[kw] + t[3 + kw] + above(t[6 + kw]) for kw in range(3)]
            else:
                r = [below(t[kw]) + t[3 + kw] + t[6 + kw] for kw in range(3)]
            planes.append(r[0] + r[1] + before(r[2]))
            planes.append(after(r[0]) + r[1] + r[2])
        return planes

    gather_finish(0)

    rows_wait(0)
    pieces = [chunk_swap([got_c[8 * half + j].astype(jnp.float32) for j in range(8)], chunk[:8]) for half in range(2)]
    values_c = jnp.concatenate(
        [
            jnp.concatenate([pieces[half][2 * quarter + frame] for quarter in range(4)], axis=0)
            for frame in range(2)
            for half in range(2)
        ],
        axis=1,
    )
    frames_start(0, row_of((row_sum(values_c), row_sum(values_c * values_c)), diagonal))
    rows_send(1)
    got_f[row] = sent_f[pl.ds(pl.multiple_of(row * width, width), width), :]

    loads[0].wait()
    gathered = cot[...].reshape(2 * n_rows * 16, cot.shape[3])
    nt = (((1,), (1,)), ((), ()))
    prod[...] = lax.dot_general(weights_c[...], gathered, nt, preferred_element_type=jnp.float32)
    halo_out_c[:, 0:cells] = coarse_frame(0).astype(halo_out_c.dtype)
    halo_out_c[:, cells:] = coarse_frame(1).astype(halo_out_c.dtype)
    halo_send(0)
    conv_c = jnp.concatenate([coarse_frame(2), coarse_frame(3)], axis=1)
    picked = one_hot(wide)
    cot_c = lax.dot_general(picked, gathered, nt, preferred_element_type=jnp.float32)

    entries_c = 16 * 2 * n_frames * cells
    entries_f = 4 * entries_c

    def norm_of(moments, entries):
        mean = group_total(column_of(moments, diagonal, 0)) / entries
        square = group_total(column_of(moments, diagonal, 1)) / entries
        return mean, lax.rsqrt(square - mean * mean + EPSILON)

    def through(values, gain, bias, mean, inv):
        normed = (values - mean) * inv
        pre = gain * normed + bias
        squash = jax.nn.sigmoid(pre)
        return normed, squash * (1.0 + pre * (1.0 - squash))

    mean_c, inv_c = norm_of(frames_total(0), entries_c)
    normed_c, slope_c = through(values_c, gain_c, bias_c, mean_c, inv_c)

    halo_wait(0)
    pre_grad_c = (conv_c + halo_in_c[...].astype(jnp.float32)) * slope_c
    frames_start(1, row_of((row_sum(pre_grad_c), row_sum(pre_grad_c * normed_c)), diagonal))
    totals_c = frames_total(1)
    one_c, two_c = column_of(totals_c, diagonal, 0), column_of(totals_c, diagonal, 1)

    def level(cot, normed, pre_grad, gain, inv, one, two, entries):
        group_one = group_total(gain * one) / entries
        group_two = group_total(gain * two) / entries
        return cot + inv * (gain * pre_grad - group_one - normed * group_two)

    level_c = level(cot_c, normed_c, pre_grad_c, gain_c, inv_c, one_c, two_c, entries_c)
    quarter = (level_c * 0.25).astype(jnp.bfloat16)
    quart[row] = quarter
    gather_start(1)

    rows_wait(1)
    swapped = []
    for half in range(2):
        swapped.append(chunk_swap([got_f[8 * half + j].astype(jnp.float32) for j in range(8)], chunk))
    values_f = jnp.concatenate([swapped[half][c] for c in range(8) for half in range(2)], axis=1)
    frames_start(2, row_of((row_sum(values_f), row_sum(values_f * values_f)), diagonal))
    gather_finish(1)

    loads[1].wait()
    prod[...] = jnp.dot(
        weights_f[...], quart[...].reshape(n_rows * width, 2 * cells), preferred_element_type=jnp.float32
    )
    for which in range(2):
        halo_out_f[:, which * 4 * cells : (which + 1) * 4 * cells] = jnp.concatenate(
            fine_frame(which), axis=1
        ).astype(halo_out_f.dtype)
    halo_send(1)
    conv_f = jnp.concatenate(fine_frame(2) + fine_frame(3), axis=1)
    mean_f, inv_f = norm_of(frames_total(2), entries_f)
    normed_f, slope_f = through(values_f, gain_f, bias_f, mean_f, inv_f)
    halo_wait(1)
    pre_grad_f = (conv_f + halo_in_f[...].astype(jnp.float32)) * slope_f
    frames_start(3, row_of((row_sum(pre_grad_f), row_sum(pre_grad_f * normed_f)), diagonal))
    totals_f = frames_total(3)
    one_f, two_f = column_of(totals_f, diagonal, 0), column_of(totals_f, diagonal, 1)

    cells_all = n_dp * 2 * n_frames * cells
    scale_c, scale_f = 1.0 / cells_all**0.5, 1.0 / (4 * cells_all) ** 0.5
    mine = row_of((two_f * scale_f, one_f * scale_f, two_c * scale_c, one_c * scale_c), diagonal)
    par_dp[dp] = mine

    def dp_copy(target, source):
        return pltpu.make_async_remote_copy(
            src_ref=par_dp.at[dp],
            dst_ref=par_dp.at[source],
            send_sem=send_dp.at[target],
            recv_sem=recv_dp.at[source],
            device_id={"dp": target},
            device_id_type=MESH,
        )

    def dp_start(d, carry):
        dp_copy(lax.rem(dp + d, n_dp), dp).start()
        return carry

    def dp_wait(d, carry):
        other = lax.rem(dp + n_dp - d, n_dp)
        dp_copy(other, other).wait_recv()
        return carry

    def dp_sent(d, carry):
        dp_copy(lax.rem(dp + d, n_dp), dp).wait_send()
        return carry

    if ring:
        pl.semaphore_wait(ready, len(ring))
    if n_dp > 1:
        lax.fori_loop(1, n_dp, dp_start, 0)

    four = [quarter[:, frame * cells : (frame + 1) * cells].astype(jnp.float32) for frame in range(2)]
    cot_f = jnp.concatenate([four[c // 4] for c in range(8)], axis=1)
    level_f = level(cot_f, normed_f, pre_grad_f, gain_f, inv_f, one_f, two_f, entries_f)
    for half in range(2):
        planes = [level_f[:, c * cells + half * LANES : c * cells + (half + 1) * LANES] for c in range(8)]
        for j, block in enumerate(chunk_swap(planes, chunk)):
            grad_out[8 * half + j] = block.astype(jnp.bfloat16)
    rows_send(2)
    grad_in[row] = grad_out[row]

    if n_dp > 1:
        lax.fori_loop(1, n_dp, dp_wait, 0)
    total = par_dp[0]
    for k in range(1, n_dp):
        total = total + par_dp[k]
    par_rows[row] = total
    rows_send(3)

    rows_wait(2)
    back = grad_in[...].reshape(n_rows * width, LANES).astype(jnp.float32).T.astype(jnp.bfloat16)
    out[...] = jnp.dot(to_old, back, preferred_element_type=jnp.float32).astype(out.dtype)

    rows_wait(3)
    lines = [jnp.concatenate([par_rows[4 * k + j] for k in range(4)], axis=0) for j in range(4)]
    part = iota(lines[0].shape, 1) >> 5
    for bit in range(2):
        step = 1 << bit
        low = ((part >> bit) & 1) == 0
        for i in range(4):
            if i & step:
                continue
            one, two = lines[i], lines[i + step]
            lines[i] = jnp.where(low, one, pltpu.roll(two, 32 * step, 1))
            lines[i + step] = jnp.where(low, pltpu.roll(one, LANES - 32 * step, 1), two)
    for k in range(4):
        par[k] = lines[k]

    gather_sent(0)
    gather_sent(1)
    for stage in range(4):
        rows_sent(stage)
    for stage in range(4):

        def frames_sent(d, carry, stage=stage):
            frames_copy(stage, lax.rem(fr + d, n_frames), fr).wait_send()
            return carry

        lax.fori_loop(1, n_frames, frames_sent, 0)

    @pl.when(fr > 0)
    def _():
        halo_copy(0).wait_send()
        halo_copy(1).wait_send()

    if n_dp > 1:
        lax.fori_loop(1, n_dp, dp_sent, 0)


def shards(
    sizes,
    acts_fine,
    acts_coarse,
    grad_coarse,
    gain_fine,
    bias_fine,
    kernel_fine,
    gain_coarse,
    bias_coarse,
    kernel_coarse,
):
    n_dp, n_frames, n_rows = sizes
    channels = acts_fine.shape[-1]
    width = channels // n_rows
    positions = 2 * n_rows * 16
    bf16, f32 = jnp.bfloat16, jnp.float32
    vmem = pl.BlockSpec(memory_space=pltpu.VMEM)
    anywhere = pl.BlockSpec(memory_space=pl.ANY)
    dma = pltpu.SemaphoreType.DMA
    taps = kernel_fine.shape[0]
    out, par = pl.pallas_call(
        functools.partial(kernel, sizes),
        out_shape=(
            jax.ShapeDtypeStruct((LANES, channels), bf16),
            jax.ShapeDtypeStruct((4, channels // LANES, LANES), f32),
        ),
        in_specs=[vmem] * 7 + [anywhere] * 2,
        out_specs=(vmem, vmem),
        scratch_shapes=[
            pltpu.VMEM((taps * width, channels), bf16),
            pltpu.VMEM((taps * width, channels), bf16),
            pltpu.VMEM((channels, LANES), bf16),
            pltpu.VMEM((n_rows, 8, LANES), bf16),
            pltpu.VMEM((n_rows, width, LANES), bf16),
            pltpu.VMEM((n_rows, 8, LANES), bf16),
            pltpu.VMEM((2, n_rows, 16, channels), bf16),
            pltpu.VMEM((n_rows, width, positions), bf16),
            pltpu.VMEM((taps * width, positions), f32),
            pltpu.VMEM((width, positions), bf16),
            pltpu.VMEM((width, positions), bf16),
            pltpu.VMEM((width, 4 * positions), bf16),
            pltpu.VMEM((width, 4 * positions), bf16),
            pltpu.VMEM((4, n_frames, 1, LANES), f32),
            pltpu.VMEM((n_dp, 1, LANES), f32),
            pltpu.VMEM((n_rows, 1, LANES), f32),
            pltpu.VMEM((n_rows, width, LANES), bf16),
            pltpu.VMEM((n_rows, width, LANES), bf16),
            dma((2,)),
            dma((4, n_rows)),
            dma((4, n_rows)),
            dma((4, n_frames)),
            dma((4, n_frames)),
            dma((2,)),
            dma((2,)),
            dma((n_dp,)),
            dma((n_dp,)),
            dma((2, 15)),
            dma((2, n_rows)),
            pltpu.SemaphoreType.REGULAR,
        ],
        compiler_params=pltpu.CompilerParams(collective_id=0, has_side_effects=True),
        name="levels",
    )(
        acts_fine.reshape(LANES, channels),
        acts_coarse.reshape(32, channels),
        grad_coarse.reshape(2, 16, channels),
        gain_fine.reshape(1, channels),
        bias_fine.reshape(1, channels),
        gain_coarse.reshape(1, channels),
        bias_coarse.reshape(1, channels),
        kernel_fine.reshape(taps * width, channels),
        kernel_coarse.reshape(taps * width, channels),
    )
    vectors = par.reshape(4, channels)
    return (out.reshape(acts_fine.shape), vectors[0], vectors[1], vectors[2], vectors[3])


def solution(mesh):
    sizes = (mesh.shape["dp"], mesh.shape["frames"], mesh.shape["rows"])
    tall = P("dp", "frames", "rows", None, None)
    in_specs = (tall, tall, tall, P(), P(), P(None, "rows", None), P(), P(), P(None, "rows", None))
    out_specs = (tall, P(), P(), P(), P())
    return jax.shard_map(
        functools.partial(shards, sizes), mesh=mesh, in_specs=in_specs, out_specs=out_specs, check_vma=False
    )
```

```python
import functools

import jax
import jax.numpy as jnp
from jax import lax
from jax.experimental import pallas as pl
from jax.experimental.pallas import tpu as pltpu
from jax.sharding import PartitionSpec as P

GROUPS = 32
EPSILON = 1e-06
MESH = pl.DeviceIdType.MESH
LANES = 128


def iota(shape, dim):
    return lax.broadcasted_iota(jnp.int32, shape, dim)


def one_hot(cond, dtype=jnp.bfloat16):
    return jnp.where(cond, 1.0, 0.0).astype(dtype)


def fine_position(new):
    frame, p, q, a, b = new >> 6, (new >> 5) & 1, (new >> 4) & 1, (new >> 3) & 1, new & 7
    return frame * 64 + (2 * a + p) * 16 + 2 * b + q


def chunk_swap(arrays, chunk):
    arrays = list(arrays)
    for bit in range(3):
        step = 1 << bit
        low = ((chunk >> bit) & 1) == 0
        for i in range(8):
            if i & step:
                continue
            one, two = arrays[i], arrays[i + step]
            arrays[i] = jnp.where(low, one, pltpu.roll(two, 16 * step, 1))
            arrays[i + step] = jnp.where(low, pltpu.roll(one, LANES - 16 * step, 1), two)
    return arrays


def group_total(column):
    per_group = column.shape[0] // 2
    split = column.reshape(2, per_group, 1)
    return jnp.broadcast_to(jnp.sum(split, axis=1, keepdims=True), split.shape).reshape(column.shape)


def row_of(columns, diagonal):
    spread = jnp.zeros(diagonal.shape, jnp.float32)
    for k, column in enumerate(columns):
        spread = jnp.where(diagonal == k, column, spread)
    return jnp.sum(spread, axis=0, keepdims=True)


def column_of(row, diagonal, k):
    return row_sum(jnp.where(diagonal == k, row, 0.0))


def row_sum(x):
    return jnp.sum(x, axis=1, keepdims=True)


def kernel(
    sizes,
    acts_fine_hbm,
    acts_coarse_hbm,
    grad_coarse_hbm,
    gain_fine_hbm,
    bias_fine_hbm,
    gain_coarse_hbm,
    bias_coarse_hbm,
    kernel_fine,
    kernel_coarse,
    out,
    par,
    acts_fine,
    acts_coarse,
    vectors,
    weights_f,
    weights_c,
    sent_f,
    sent_c,
    got_f,
    got_c,
    cot,
    quart,
    prod,
    halo_out_c,
    halo_in_c,
    halo_out_f,
    halo_in_f,
    stats,
    par_z,
    par_xy,
    grad_out,
    grad_in,
    load_sem,
    send_rows,
    recv_rows,
    send_frames,
    recv_frames,
    send_halo,
    recv_halo,
    par_sem,
    send_relay,
    recv_relay,
    ready,
):
    n_dp, n_frames, n_rows = sizes
    dp, fr, row = lax.axis_index("dp"), lax.axis_index("frames"), lax.axis_index("rows")
    width = weights_f.shape[0] // 27

    loads = [
        pltpu.make_async_copy(grad_coarse_hbm, cot.at[:, row], load_sem.at[0]),
        pltpu.make_async_copy(acts_coarse_hbm, acts_coarse, load_sem.at[1]),
        pltpu.make_async_copy(acts_fine_hbm, acts_fine, load_sem.at[2]),
        pltpu.make_async_copy(gain_fine_hbm, vectors.at[0], load_sem.at[3]),
        pltpu.make_async_copy(bias_fine_hbm, vectors.at[1], load_sem.at[3]),
        pltpu.make_async_copy(gain_coarse_hbm, vectors.at[2], load_sem.at[3]),
        pltpu.make_async_copy(bias_coarse_hbm, vectors.at[3], load_sem.at[3]),
        pltpu.make_async_copy(kernel_coarse, weights_c, load_sem.at[4]),
        pltpu.make_async_copy(kernel_fine, weights_f, load_sem.at[5]),
    ]
    loads[0].start()

    even = dp + 1 - 2 * lax.rem(dp, 2)
    near_dp = [even] + [lax.rem(core + step, n_dp) for core in (dp, even) for step in (2, n_dp - 2)]
    barrier = pltpu.get_barrier_semaphore()
    for axis, me, count in (("rows", row, n_rows), ("frames", fr, n_frames)):

        def greet(d, carry, axis=axis, me=me, count=count):
            pl.semaphore_signal(barrier, inc=1, device_id={axis: lax.rem(me + d, count)}, device_id_type=MESH)
            return carry

        lax.fori_loop(1, count, greet, 0)
    for peer in near_dp:
        pl.semaphore_signal(barrier, inc=1, device_id={"dp": peer}, device_id_type=MESH)

    for load in loads[1:]:
        load.start()

    loads[1].wait()
    place, source = iota((LANES, 32), 0), iota((LANES, 32), 1)
    placed = jnp.dot(one_hot((place & 31) == source), acts_coarse[...], preferred_element_type=jnp.float32)
    quads = placed.T.reshape(n_rows, 4, 8, LANES)
    quad = iota((n_rows, 8, LANES), 2) >> 5
    folded = jnp.where(quad == 0, quads[:, 0], 0.0)
    for k in range(1, 4):
        folded = jnp.where(quad == k, quads[:, k], folded)
    sent_c[...] = folded.astype(jnp.bfloat16)

    loads[0].wait()
    pl.semaphore_wait(barrier, (n_rows - 1) + (n_frames - 1) + len(near_dp))

    def tell(round_):
        for peer in near_dp:
            pl.semaphore_signal(ready.at[round_], inc=1, device_id={"dp": peer}, device_id_type=MESH)

    def told(round_):
        if near_dp:
            pl.semaphore_wait(ready.at[round_], len(near_dp))

    def all_of(ref, sem):
        pltpu.make_async_copy(ref, ref, sem).wait()

    def slices(ref, index):
        return ref.at[pl.ds(pl.multiple_of(index * width, width), width)]

    def rows_copy(stage, target, source):
        if stage == 0:
            src, dst = sent_c.at[target], got_c.at[source]
        elif stage == 1:
            src, dst = slices(sent_f, target), got_f.at[source]
        else:
            src, dst = grad_out.at[target], grad_in.at[source]
        return pltpu.make_async_remote_copy(
            src_ref=src,
            dst_ref=dst,
            send_sem=send_rows.at[stage],
            recv_sem=recv_rows.at[stage],
            device_id={"rows": target},
            device_id_type=MESH,
        )

    y, z = lax.div(row, 4), lax.rem(row, 4)
    z_mate = (z, z + 1 - 2 * lax.rem(z, 2), lax.rem(z + 2, 4), 3 - z)
    y_up, y_down, y_far = lax.rem(y + 1, 4), lax.rem(y + 3, 4), lax.rem(y + 2, 4)

    def at(y_of, z_of):
        return 4 * y_of + z_of

    def relay(stage, kind, slot, target):
        block = (cot.at[:, slot], quart.at[slot])[stage]
        return pltpu.make_async_remote_copy(
            src_ref=block,
            dst_ref=block,
            send_sem=send_relay.at[stage],
            recv_sem=recv_relay.at[stage, kind],
            device_id={"rows": target},
            device_id_type=MESH,
        )

    up, down = at(y_up, z), at(y_down, z)
    z_kind, up_kind, down_kind = (None, 0, 2, 4), (1, 7, 5, 7), (7, 3, 7, 6)

    def gather_start(stage):
        relay(stage, z_kind[1], row, at(y, z_mate[1])).start()
        relay(stage, up_kind[0], row, up).start()
        relay(stage, down_kind[0], row, down).start()
        relay(stage, z_kind[2], row, at(y, z_mate[2])).start()
        relay(stage, z_kind[3], row, at(y, z_mate[3])).start()

    def gather_relay(stage):
        for kind, y_of, j in ((0, y, 1), (1, y_down, 0), (2, y, 2), (3, y_up, 1), (4, y, 3), (5, y_down, 2), (6, y_up, 3)):
            slot = at(y_of, z_mate[j])
            relay(stage, kind, slot, row).wait_recv()
            if kind in (0, 2, 4):
                relay(stage, up_kind[j], slot, up).start()
                relay(stage, down_kind[j], slot, down).start()
            elif kind in (1, 5):
                relay(stage, 7, slot, up).start()
            else:
                relay(stage, 7, slot, down).start()

    def gather_finish(stage):
        all_of((cot.at[:, pl.ds(0, 8)], quart.at[pl.ds(0, 8)])[stage], recv_relay.at[stage, 7])

    def gather_sent(stage):
        all_of((cot.at[:, pl.ds(0, 15)], quart.at[pl.ds(0, 15)])[stage], send_relay.at[stage])

    def rows_send(stage):
        def step(d, carry):
            rows_copy(stage, lax.rem(row + d, n_rows), row).start()
            return carry

        lax.fori_loop(1, n_rows, step, 0)

    def rows_refs(stage):
        return (got_c, got_f, grad_in)[stage].at[pl.ds(0, n_rows - 1)]

    def rows_wait(stage):
        all_of(rows_refs(stage), recv_rows.at[stage])

    def rows_sent(stage):
        all_of(rows_refs(stage), send_rows.at[stage])

    def frames_copy(stage, target, source):
        return pltpu.make_async_remote_copy(
            src_ref=stats.at[stage, fr],
            dst_ref=stats.at[stage, source],
            send_sem=send_frames.at[stage],
            recv_sem=recv_frames.at[stage],
            device_id={"frames": target},
            device_id_type=MESH,
        )

    def frames_start(stage, block):
        stats[stage, fr] = block

        def step(d, carry):
            frames_copy(stage, lax.rem(fr + d, n_frames), fr).start()
            return carry

        lax.fori_loop(1, n_frames, step, 0)

    def frames_total(stage):
        all_of(stats.at[stage, pl.ds(0, n_frames - 1)], recv_frames.at[stage])
        total = stats[stage, 0]
        for k in range(1, n_frames):
            total = total + stats[stage, k]
        return total

    def halo_copy(stage):
        src, dst = ((halo_out_c, halo_in_c), (halo_out_f, halo_in_f))[stage]
        return pltpu.make_async_remote_copy(
            src_ref=src,
            dst_ref=dst,
            send_sem=send_halo.at[stage],
            recv_sem=recv_halo.at[stage],
            device_id={"frames": lax.rem(fr + n_frames - 1, n_frames)},
            device_id_type=MESH,
        )

    def halo_send(stage):
        @pl.when(fr > 0)
        def _():
            halo_copy(stage).start()

    def halo_wait(stage):
        @pl.when(fr < n_frames - 1)
        def _():
            halo_copy(stage).wait_recv()

        @pl.when(fr == n_frames - 1)
        def _():
            into = (halo_in_c, halo_in_f)[stage]
            into[...] = jnp.zeros_like(into)

    gather_start(0)
    rows_send(0)
    got_c[row] = sent_c[row]
    tell(0)

    loads[2].wait()
    new, old = iota((LANES, LANES), 0), iota((LANES, LANES), 1)
    to_new = one_hot(old == fine_position(new))
    to_old = one_hot(new == fine_position(old))
    moved = jnp.dot(to_new, acts_fine[...], preferred_element_type=jnp.float32)
    sent_f[...] = moved.T.astype(jnp.bfloat16)
    all_of(vectors, load_sem.at[3])

    wide = iota((width, vectors.shape[2]), 1) == row * width + iota((width, vectors.shape[2]), 0)

    def column(vector):
        return row_sum(jnp.where(wide, vector, 0.0))

    gain_f, bias_f, gain_c, bias_c = (column(vectors[k]) for k in range(4))
    lane, channel = iota((width, LANES), 1), iota((width, LANES), 0)
    chunk = lane >> 4
    diagonal = jnp.where((lane & 31) == channel, lane >> 5, -1)

    cells = 256
    spot = iota((width, cells), 1)
    top, bottom = spot >= 8, spot < cells - 8
    left, right = (spot & 7) > 0, (spot & 7) < 7

    def above(x):
        return jnp.where(top, pltpu.roll(x, 8, 1), 0.0)

    def below(x):
        return jnp.where(bottom, pltpu.roll(x, cells - 8, 1), 0.0)

    def before(x):
        return jnp.where(left, pltpu.roll(x, 1, 1), 0.0)

    def after(x):
        return jnp.where(right, pltpu.roll(x, cells - 1, 1), 0.0)

    def product(depth, tap, frame):
        at = (depth * 9 + tap) * width
        return prod[at : at + width, frame * cells : (frame + 1) * cells]

    def spatial_taps(which):
        terms = (((0, 0),), ((1, 0), (0, 1)), ((2, 0), (1, 1)), ((2, 1),))[which]
        taps = []
        for tap in range(9):
            total = product(terms[0][0], tap, terms[0][1])
            for depth, frame in terms[1:]:
                total = total + product(depth, tap, frame)
            taps.append(total)
        return taps

    def coarse_frame(which):
        t = spatial_taps(which)
        r = [below(t[kw]) + t[3 + kw] + above(t[6 + kw]) for kw in range(3)]
        return after(r[0]) + r[1] + before(r[2])

    def fine_frame(which):
        t = spatial_taps(which)
        planes = []
        for p in range(2):
            if p == 0:
                r = [t[kw] + t[3 + kw] + above(t[6 + kw]) for kw in range(3)]
            else:
                r = [below(t[kw]) + t[3 + kw] + t[6 + kw] for kw in range(3)]
            planes.append(r[0] + r[1] + before(r[2]))
            planes.append(after(r[0]) + r[1] + r[2])
        return planes

    gather_relay(0)

    rows_wait(0)
    pieces = [chunk_swap([got_c[8 * half + j].astype(jnp.float32) for j in range(8)], chunk[:8]) for half in range(2)]
    values_c = jnp.concatenate(
        [
            jnp.concatenate([pieces[half][2 * quarter + frame] for quarter in range(4)], axis=0)
            for frame in range(2)
            for half in range(2)
        ],
        axis=1,
    )
    frames_start(0, row_of((row_sum(values_c), row_sum(values_c * values_c)), diagonal))
    rows_send(1)
    got_f[row] = sent_f[pl.ds(pl.multiple_of(row * width, width), width), :]

    loads[7].wait()
    told(0)
    tell(1)
    gather_finish(0)
    gathered = cot[...].reshape(2 * n_rows * 16, cot.shape[3])
    nt = (((1,), (1,)), ((), ()))
    prod[...] = lax.dot_general(weights_c[...], gathered, nt, preferred_element_type=jnp.float32)
    halo_out_c[:, 0:cells] = coarse_frame(0).astype(halo_out_c.dtype)
    halo_out_c[:, cells:] = coarse_frame(1).astype(halo_out_c.dtype)
    halo_send(0)
    conv_c = jnp.concatenate([coarse_frame(2), coarse_frame(3)], axis=1)
    picked = one_hot(wide)
    cot_c = lax.dot_general(picked, gathered, nt, preferred_element_type=jnp.float32)

    entries_c = 16 * 2 * n_frames * cells
    entries_f = 4 * entries_c

    def norm_of(moments, entries):
        mean = group_total(column_of(moments, diagonal, 0)) / entries
        square = group_total(column_of(moments, diagonal, 1)) / entries
        return mean, lax.rsqrt(square - mean * mean + EPSILON)

    def through(values, gain, bias, mean, inv):
        normed = (values - mean) * inv
        pre = gain * normed + bias
        squash = jax.nn.sigmoid(pre)
        return normed, squash * (1.0 + pre * (1.0 - squash))

    mean_c, inv_c = norm_of(frames_total(0), entries_c)
    normed_c, slope_c = through(values_c, gain_c, bias_c, mean_c, inv_c)

    halo_wait(0)
    pre_grad_c = (conv_c + halo_in_c[...].astype(jnp.float32)) * slope_c
    here_c = (row_sum(pre_grad_c), row_sum(pre_grad_c * normed_c))
    frames_start(1, row_of(here_c, diagonal))
    totals_c = frames_total(1)
    one_c, two_c = column_of(totals_c, diagonal, 0), column_of(totals_c, diagonal, 1)

    def level(cot, normed, pre_grad, gain, inv, one, two, entries):
        group_one = group_total(gain * one) / entries
        group_two = group_total(gain * two) / entries
        return cot + inv * (gain * pre_grad - group_one - normed * group_two)

    level_c = level(cot_c, normed_c, pre_grad_c, gain_c, inv_c, one_c, two_c, entries_c)
    quarter = (level_c * 0.25).astype(jnp.bfloat16)
    quart[row] = quarter
    gather_start(1)
    gather_relay(1)

    rows_wait(1)
    swapped = []
    for half in range(2):
        swapped.append(chunk_swap([got_f[8 * half + j].astype(jnp.float32) for j in range(8)], chunk))
    values_f = jnp.concatenate([swapped[half][c] for c in range(8) for half in range(2)], axis=1)
    frames_start(2, row_of((row_sum(values_f), row_sum(values_f * values_f)), diagonal))
    gather_finish(1)

    loads[8].wait()
    prod[...] = jnp.dot(
        weights_f[...], quart[...].reshape(n_rows * width, 2 * cells), preferred_element_type=jnp.float32
    )
    for which in range(2):
        halo_out_f[:, which * 4 * cells : (which + 1) * 4 * cells] = jnp.concatenate(
            fine_frame(which), axis=1
        ).astype(halo_out_f.dtype)
    halo_send(1)
    conv_f = jnp.concatenate(fine_frame(2) + fine_frame(3), axis=1)
    mean_f, inv_f = norm_of(frames_total(2), entries_f)
    normed_f, slope_f = through(values_f, gain_f, bias_f, mean_f, inv_f)
    halo_wait(1)
    pre_grad_f = (conv_f + halo_in_f[...].astype(jnp.float32)) * slope_f
    here_f = (row_sum(pre_grad_f), row_sum(pre_grad_f * normed_f))
    frames_start(3, row_of(here_f, diagonal))

    cells_all = n_dp * 2 * n_frames * cells
    scale_c, scale_f = 1.0 / cells_all**0.5, 1.0 / (4 * cells_all) ** 0.5
    n_z, n_xy = 4 * n_dp, 4 * n_frames
    in_z, in_xy = 4 * dp + z, 4 * fr + y

    def z_copy(target, source):
        return pltpu.make_async_remote_copy(
            src_ref=par_z.at[in_z],
            dst_ref=par_z.at[source],
            send_sem=par_sem.at[0],
            recv_sem=par_sem.at[1],
            device_id={"dp": lax.div(target, 4), "rows": 4 * y + lax.rem(target, 4)},
            device_id_type=MESH,
        )

    def xy_copy(target, source):
        return pltpu.make_async_remote_copy(
            src_ref=par_xy.at[in_xy],
            dst_ref=par_xy.at[source],
            send_sem=par_sem.at[2],
            recv_sem=par_sem.at[3],
            device_id={"frames": lax.div(target, 4), "rows": 4 * lax.rem(target, 4) + z},
            device_id_type=MESH,
        )

    def each(count, body):
        def step(d, carry):
            body(d)
            return carry

        lax.fori_loop(1, count, step, 0)

    mine = (here_f[1] * scale_f, here_f[0] * scale_f, here_c[1] * scale_c, here_c[0] * scale_c)
    par_z[in_z] = row_of(mine, diagonal)
    told(1)
    each(n_z, lambda d: z_copy(lax.rem(in_z + d, n_z), in_z).start())

    totals_f = frames_total(3)
    one_f, two_f = column_of(totals_f, diagonal, 0), column_of(totals_f, diagonal, 1)

    four = [quarter[:, frame * cells : (frame + 1) * cells].astype(jnp.float32) for frame in range(2)]
    cot_f = jnp.concatenate([four[c // 4] for c in range(8)], axis=1)
    level_f = level(cot_f, normed_f, pre_grad_f, gain_f, inv_f, one_f, two_f, entries_f)
    for half in range(2):
        planes = [level_f[:, c * cells + half * LANES : c * cells + (half + 1) * LANES] for c in range(8)]
        for j, block in enumerate(chunk_swap(planes, chunk)):
            grad_out[8 * half + j] = block.astype(jnp.bfloat16)
    rows_send(2)
    grad_in[row] = grad_out[row]

    gather_sent(0)
    gather_sent(1)
    for stage in range(2):
        rows_sent(stage)
    for stage in range(4):
        all_of(stats.at[stage, pl.ds(0, n_frames - 1)], send_frames.at[stage])

    @pl.when(fr > 0)
    def _():
        halo_copy(0).wait_send()
        halo_copy(1).wait_send()

    all_of(par_z.at[pl.ds(0, n_z - 1)], par_sem.at[1])
    for k in range(4):
        total = par_z[k]
        for j in range(1, n_dp):
            total = total + par_z[4 * j + k]
        par_xy[in_xy, k : k + 1] = total
    each(n_xy, lambda d: xy_copy(lax.rem(in_xy + d, n_xy), in_xy).start())

    rows_wait(2)
    back = grad_in[...].reshape(n_rows * width, LANES).astype(jnp.float32).T.astype(jnp.bfloat16)
    out[...] = jnp.dot(to_old, back, preferred_element_type=jnp.float32).astype(out.dtype)

    rows_sent(2)
    all_of(par_z.at[pl.ds(0, n_z - 1)], par_sem.at[0])
    all_of(par_xy.at[pl.ds(0, n_xy - 1)], par_sem.at[3])
    sums = []
    for k in range(4):
        total = par_xy[k]
        for j in range(1, n_frames):
            total = total + par_xy[4 * j + k]
        sums.append(total)
    lines = [jnp.concatenate([sums[k][j : j + 1] for k in range(4)], axis=0) for j in range(4)]
    part = iota(lines[0].shape, 1) >> 5
    for bit in range(2):
        step = 1 << bit
        low = ((part >> bit) & 1) == 0
        for i in range(4):
            if i & step:
                continue
            one, two = lines[i], lines[i + step]
            lines[i] = jnp.where(low, one, pltpu.roll(two, 32 * step, 1))
            lines[i + step] = jnp.where(low, pltpu.roll(one, LANES - 32 * step, 1), two)
    for k in range(4):
        par[k] = lines[k]

    all_of(par_xy.at[pl.ds(0, n_xy - 1)], par_sem.at[2])


def finish(grad, par, out, *vectors):
    out[...] = grad[...]
    for k, vector in enumerate(vectors):
        vector[...] = par[k]


def shards(
    sizes,
    acts_fine,
    acts_coarse,
    grad_coarse,
    gain_fine,
    bias_fine,
    kernel_fine,
    gain_coarse,
    bias_coarse,
    kernel_coarse,
):
    n_dp, n_frames, n_rows = sizes
    channels = acts_fine.shape[-1]
    width = channels // n_rows
    positions = 2 * n_rows * 16
    bf16, f32 = jnp.bfloat16, jnp.float32
    vmem = pl.BlockSpec(memory_space=pltpu.VMEM)
    anywhere = pl.BlockSpec(memory_space=pl.ANY)
    dma = pltpu.SemaphoreType.DMA
    taps = kernel_fine.shape[0]
    held = (pltpu.VMEM((LANES, channels), bf16), pltpu.VMEM((4, channels // LANES, LANES), f32))
    out, par = pl.pallas_call(
        functools.partial(kernel, sizes),
        out_shape=held,
        in_specs=[anywhere] * 9,
        out_specs=(vmem, vmem),
        scratch_shapes=[
            pltpu.VMEM((LANES, channels), bf16),
            pltpu.VMEM((32, channels), bf16),
            pltpu.VMEM((4, 1, channels), f32),
            pltpu.VMEM((taps * width, channels), bf16),
            pltpu.VMEM((taps * width, channels), bf16),
            pltpu.VMEM((channels, LANES), bf16),
            pltpu.VMEM((n_rows, 8, LANES), bf16),
            pltpu.VMEM((n_rows, width, LANES), bf16),
            pltpu.VMEM((n_rows, 8, LANES), bf16),
            pltpu.VMEM((2, n_rows, 16, channels), bf16),
            pltpu.VMEM((n_rows, width, positions), bf16),
            pltpu.VMEM((taps * width, positions), f32),
            pltpu.VMEM((width, positions), bf16),
            pltpu.VMEM((width, positions), bf16),
            pltpu.VMEM((width, 4 * positions), bf16),
            pltpu.VMEM((width, 4 * positions), bf16),
            pltpu.VMEM((4, n_frames, 1, LANES), f32),
            pltpu.VMEM((4 * n_dp, 1, LANES), f32),
            pltpu.VMEM((4 * n_frames, 4, LANES), f32),
            pltpu.VMEM((n_rows, width, LANES), bf16),
            pltpu.VMEM((n_rows, width, LANES), bf16),
            dma((6,)),
            dma((3,)),
            dma((3,)),
            dma((4,)),
            dma((4,)),
            dma((2,)),
            dma((2,)),
            dma((4,)),
            dma((2,)),
            dma((2, 8)),
            pltpu.SemaphoreType.REGULAR((2,)),
        ],
        compiler_params=pltpu.CompilerParams(collective_id=0, has_side_effects=True),
        name="levels",
    )(
        acts_fine.reshape(LANES, channels),
        acts_coarse.reshape(32, channels),
        grad_coarse.reshape(2, 16, channels),
        gain_fine.reshape(1, channels),
        bias_fine.reshape(1, channels),
        gain_coarse.reshape(1, channels),
        bias_coarse.reshape(1, channels),
        kernel_fine.reshape(taps * width, channels),
        kernel_coarse.reshape(taps * width, channels),
    )
    vector = jax.ShapeDtypeStruct((channels // LANES, LANES), f32)
    grad, *vectors = pl.pallas_call(
        finish,
        out_shape=(jax.ShapeDtypeStruct((LANES, channels), bf16), vector, vector, vector, vector),
        in_specs=[vmem, vmem],
        out_specs=(vmem,) * 5,
        name="finish",
    )(*(pltpu.with_memory_space_constraint(x, pltpu.VMEM) for x in (out, par)))
    return (grad.reshape(acts_fine.shape), *(v.reshape(channels) for v in vectors))


def solution(mesh):
    sizes = (mesh.shape["dp"], mesh.shape["frames"], mesh.shape["rows"])
    tall = P("dp", "frames", "rows", None, None)
    in_specs = (tall, tall, tall, P(), P(), P(None, "rows", None), P(), P(), P(None, "rows", None))
    out_specs = (tall, P(), P(), P(), P())
    return jax.shard_map(
        functools.partial(shards, sizes), mesh=mesh, in_specs=in_specs, out_specs=out_specs, check_vma=False
    )
```

```python
import functools

import jax
import jax.numpy as jnp
from jax import lax
from jax.experimental import pallas as pl
from jax.experimental.pallas import tpu as pltpu
from jax.sharding import PartitionSpec as P

GROUPS = 32
EPSILON = 1e-06
MESH = pl.DeviceIdType.MESH
LANES = 128


def iota(shape, dim):
    return lax.broadcasted_iota(jnp.int32, shape, dim)


def one_hot(cond, dtype=jnp.bfloat16):
    return jnp.where(cond, 1.0, 0.0).astype(dtype)


def fine_position(new):
    frame, p, q, a, b = new >> 6, (new >> 5) & 1, (new >> 4) & 1, (new >> 3) & 1, new & 7
    return frame * 64 + (2 * a + p) * 16 + 2 * b + q


def chunk_swap(arrays, chunk):
    arrays = list(arrays)
    for bit in range(3):
        step = 1 << bit
        low = ((chunk >> bit) & 1) == 0
        for i in range(8):
            if i & step:
                continue
            one, two = arrays[i], arrays[i + step]
            arrays[i] = jnp.where(low, one, pltpu.roll(two, 16 * step, 1))
            arrays[i + step] = jnp.where(low, pltpu.roll(one, LANES - 16 * step, 1), two)
    return arrays


def group_total(column):
    per_group = column.shape[0] // 2
    split = column.reshape(2, per_group, 1)
    return jnp.broadcast_to(jnp.sum(split, axis=1, keepdims=True), split.shape).reshape(column.shape)


def row_of(columns, diagonal):
    spread = jnp.zeros(diagonal.shape, jnp.float32)
    for k, column in enumerate(columns):
        spread = jnp.where(diagonal == k, column, spread)
    return jnp.sum(spread, axis=0, keepdims=True)


def column_of(row, diagonal, k):
    return row_sum(jnp.where(diagonal == k, row, 0.0))


def row_sum(x):
    return jnp.sum(x, axis=1, keepdims=True)


def kernel(
    sizes,
    acts_fine_hbm,
    acts_coarse_hbm,
    grad_coarse_hbm,
    gain_fine_hbm,
    bias_fine_hbm,
    gain_coarse_hbm,
    bias_coarse_hbm,
    kernel_fine,
    kernel_coarse,
    out,
    par,
    acts_fine,
    acts_coarse,
    vectors,
    weights_f,
    weights_c,
    sent_f,
    sent_c,
    got_f,
    got_c,
    cot,
    quart,
    prod,
    halo_out_c,
    halo_in_c,
    halo_out_f,
    halo_in_f,
    here_vals_c,
    prev_vals_c,
    here_vals_f,
    prev_vals_f,
    stats,
    par_z,
    par_xy,
    grad_out,
    grad_in,
    load_sem,
    send_rows,
    recv_rows,
    send_frames,
    recv_frames,
    send_halo,
    recv_halo,
    pass_sem,
    par_sem,
    send_relay,
    recv_relay,
    ready,
):
    n_dp, n_frames, n_rows = sizes
    dp, fr, row = lax.axis_index("dp"), lax.axis_index("frames"), lax.axis_index("rows")
    width = weights_f.shape[0] // 27

    loads = [
        pltpu.make_async_copy(grad_coarse_hbm, cot.at[:, row], load_sem.at[0]),
        pltpu.make_async_copy(acts_coarse_hbm, acts_coarse, load_sem.at[1]),
        pltpu.make_async_copy(acts_fine_hbm, acts_fine, load_sem.at[2]),
        pltpu.make_async_copy(gain_fine_hbm, vectors.at[0], load_sem.at[3]),
        pltpu.make_async_copy(bias_fine_hbm, vectors.at[1], load_sem.at[3]),
        pltpu.make_async_copy(gain_coarse_hbm, vectors.at[2], load_sem.at[3]),
        pltpu.make_async_copy(bias_coarse_hbm, vectors.at[3], load_sem.at[3]),
        pltpu.make_async_copy(kernel_coarse, weights_c, load_sem.at[4]),
        pltpu.make_async_copy(kernel_fine, weights_f, load_sem.at[5]),
    ]
    loads[0].start()

    even = dp + 1 - 2 * lax.rem(dp, 2)
    near_dp = [even] + [lax.rem(core + step, n_dp) for core in (dp, even) for step in (2, n_dp - 2)]
    barrier = pltpu.get_barrier_semaphore()
    for axis, me, count in (("rows", row, n_rows), ("frames", fr, n_frames)):

        def greet(d, carry, axis=axis, me=me, count=count):
            pl.semaphore_signal(barrier, inc=1, device_id={axis: lax.rem(me + d, count)}, device_id_type=MESH)
            return carry

        lax.fori_loop(1, count, greet, 0)
    for peer in near_dp:
        pl.semaphore_signal(barrier, inc=1, device_id={"dp": peer}, device_id_type=MESH)

    for load in loads[1:]:
        load.start()

    loads[1].wait()
    place, source = iota((LANES, 32), 0), iota((LANES, 32), 1)
    placed = jnp.dot(one_hot((place & 31) == source), acts_coarse[...], preferred_element_type=jnp.float32)
    quads = placed.T.reshape(n_rows, 4, 8, LANES)
    quad = iota((n_rows, 8, LANES), 2) >> 5
    folded = jnp.where(quad == 0, quads[:, 0], 0.0)
    for k in range(1, 4):
        folded = jnp.where(quad == k, quads[:, k], folded)
    sent_c[...] = folded.astype(jnp.bfloat16)

    loads[0].wait()
    pl.semaphore_wait(barrier, (n_rows - 1) + (n_frames - 1) + len(near_dp))

    def tell(round_):
        for peer in near_dp:
            pl.semaphore_signal(ready.at[round_], inc=1, device_id={"dp": peer}, device_id_type=MESH)

    def told(round_):
        if near_dp:
            pl.semaphore_wait(ready.at[round_], len(near_dp))

    def all_of(ref, sem):
        pltpu.make_async_copy(ref, ref, sem).wait()

    def slices(ref, index):
        return ref.at[pl.ds(pl.multiple_of(index * width, width), width)]

    def rows_copy(stage, target, source):
        if stage == 0:
            src, dst = sent_c.at[target], got_c.at[source]
        elif stage == 1:
            src, dst = slices(sent_f, target), got_f.at[source]
        else:
            src, dst = grad_out.at[target], grad_in.at[source]
        return pltpu.make_async_remote_copy(
            src_ref=src,
            dst_ref=dst,
            send_sem=send_rows.at[stage],
            recv_sem=recv_rows.at[stage],
            device_id={"rows": target},
            device_id_type=MESH,
        )

    y, z = lax.div(row, 4), lax.rem(row, 4)
    z_mate = (z, z + 1 - 2 * lax.rem(z, 2), lax.rem(z + 2, 4), 3 - z)
    y_up, y_down, y_far = lax.rem(y + 1, 4), lax.rem(y + 3, 4), lax.rem(y + 2, 4)

    def at(y_of, z_of):
        return 4 * y_of + z_of

    def relay(stage, kind, slot, target):
        block = (cot.at[:, slot], quart.at[slot])[stage]
        return pltpu.make_async_remote_copy(
            src_ref=block,
            dst_ref=block,
            send_sem=send_relay.at[stage],
            recv_sem=recv_relay.at[stage, kind],
            device_id={"rows": target},
            device_id_type=MESH,
        )

    up, down = at(y_up, z), at(y_down, z)
    z_kind, up_kind, down_kind = (None, 0, 2, 4), (1, 7, 5, 7), (7, 3, 7, 6)

    def gather_start(stage):
        relay(stage, z_kind[1], row, at(y, z_mate[1])).start()
        relay(stage, up_kind[0], row, up).start()
        relay(stage, down_kind[0], row, down).start()
        relay(stage, z_kind[2], row, at(y, z_mate[2])).start()
        relay(stage, z_kind[3], row, at(y, z_mate[3])).start()

    def gather_relay(stage):
        for kind, y_of, j in ((0, y, 1), (1, y_down, 0), (2, y, 2), (4, y, 3), (3, y_up, 1), (5, y_down, 2), (6, y_up, 3)):
            slot = at(y_of, z_mate[j])
            relay(stage, kind, slot, row).wait_recv()
            if kind in (0, 2, 4):
                relay(stage, up_kind[j], slot, up).start()
                relay(stage, down_kind[j], slot, down).start()
            elif kind in (1, 5):
                relay(stage, 7, slot, up).start()
            else:
                relay(stage, 7, slot, down).start()

    def gather_finish(stage):
        all_of((cot.at[:, pl.ds(0, 8)], quart.at[pl.ds(0, 8)])[stage], recv_relay.at[stage, 7])

    def gather_sent(stage):
        all_of((cot.at[:, pl.ds(0, 15)], quart.at[pl.ds(0, 15)])[stage], send_relay.at[stage])

    def rows_send(stage):
        def step(d, carry):
            rows_copy(stage, lax.rem(row + d, n_rows), row).start()
            return carry

        lax.fori_loop(1, n_rows, step, 0)

    def rows_refs(stage):
        return (got_c, got_f, grad_in)[stage].at[pl.ds(0, n_rows - 1)]

    def rows_wait(stage):
        all_of(rows_refs(stage), recv_rows.at[stage])

    def rows_sent(stage):
        all_of(rows_refs(stage), send_rows.at[stage])

    def frames_copy(stage, target, source):
        return pltpu.make_async_remote_copy(
            src_ref=stats.at[stage, fr],
            dst_ref=stats.at[stage, source],
            send_sem=send_frames.at[stage],
            recv_sem=recv_frames.at[stage],
            device_id={"frames": target},
            device_id_type=MESH,
        )

    def frames_start(stage, block):
        stats[stage, fr] = block

        def step(d, carry):
            frames_copy(stage, lax.rem(fr + d, n_frames), fr).start()
            return carry

        lax.fori_loop(1, n_frames, step, 0)

    def frames_total(stage):
        all_of(stats.at[stage, pl.ds(0, n_frames - 1)], recv_frames.at[stage])
        total = stats[stage, 0]
        for k in range(1, n_frames):
            total = total + stats[stage, k]
        return total

    def halo_copy(stage):
        src, dst = ((halo_out_c, halo_in_c), (halo_out_f, halo_in_f))[stage]
        return pltpu.make_async_remote_copy(
            src_ref=src,
            dst_ref=dst,
            send_sem=send_halo.at[stage],
            recv_sem=recv_halo.at[stage],
            device_id={"frames": lax.rem(fr + n_frames - 1, n_frames)},
            device_id_type=MESH,
        )

    def halo_send(stage):
        @pl.when(fr > 0)
        def _():
            halo_copy(stage).start()

    def halo_wait(stage):
        @pl.when(fr < n_frames - 1)
        def _():
            halo_copy(stage).wait_recv()

        @pl.when(fr == n_frames - 1)
        def _():
            into = (halo_in_c, halo_in_f)[stage]
            into[...] = jnp.zeros_like(into)

    gather_start(0)
    rows_send(0)
    got_c[row] = sent_c[row]
    tell(0)

    loads[2].wait()
    new, old = iota((LANES, LANES), 0), iota((LANES, LANES), 1)
    to_new = one_hot(old == fine_position(new))
    to_old = one_hot(new == fine_position(old))
    moved = jnp.dot(to_new, acts_fine[...], preferred_element_type=jnp.float32)
    sent_f[...] = moved.T.astype(jnp.bfloat16)
    all_of(vectors, load_sem.at[3])

    def pass_on(stage):
        here, there = ((here_vals_c, prev_vals_c), (here_vals_f, prev_vals_f))[stage]
        return pltpu.make_async_remote_copy(
            src_ref=here,
            dst_ref=there,
            send_sem=pass_sem.at[0, stage],
            recv_sem=pass_sem.at[1, stage],
            device_id={"frames": lax.rem(fr + 1, n_frames)},
            device_id_type=MESH,
        )

    def pass_send(stage):
        @pl.when(fr < n_frames - 1)
        def _():
            pass_on(stage).start()

    def pass_wait(stage):
        @pl.when(fr > 0)
        def _():
            pass_on(stage).wait_recv()

        @pl.when(fr == 0)
        def _():
            into = (prev_vals_c, prev_vals_f)[stage]
            into[...] = jnp.zeros_like(into)

    wide = iota((width, vectors.shape[2]), 1) == row * width + iota((width, vectors.shape[2]), 0)

    def column(vector):
        return row_sum(jnp.where(wide, vector, 0.0))

    gain_f, bias_f, gain_c, bias_c = (column(vectors[k]) for k in range(4))
    lane, channel = iota((width, LANES), 1), iota((width, LANES), 0)
    chunk = lane >> 4
    diagonal = jnp.where((lane & 31) == channel, lane >> 5, -1)

    cells = 256
    spot = iota((width, cells), 1)
    top, bottom = spot >= 8, spot < cells - 8
    left, right = (spot & 7) > 0, (spot & 7) < 7

    def above(x):
        return jnp.where(top, pltpu.roll(x, 8, 1), 0.0)

    def below(x):
        return jnp.where(bottom, pltpu.roll(x, cells - 8, 1), 0.0)

    def before(x):
        return jnp.where(left, pltpu.roll(x, 1, 1), 0.0)

    def after(x):
        return jnp.where(right, pltpu.roll(x, cells - 1, 1), 0.0)

    def product(depth, tap, frame):
        at = (depth * 9 + tap) * width
        return prod[at : at + width, frame * cells : (frame + 1) * cells]

    def spatial_taps(which):
        terms = (((0, 0),), ((1, 0), (0, 1)), ((2, 0), (1, 1)), ((2, 1),))[which]
        taps = []
        for tap in range(9):
            total = product(terms[0][0], tap, terms[0][1])
            for depth, frame in terms[1:]:
                total = total + product(depth, tap, frame)
            taps.append(total)
        return taps

    def coarse_frame(which):
        t = spatial_taps(which)
        r = [below(t[kw]) + t[3 + kw] + above(t[6 + kw]) for kw in range(3)]
        return after(r[0]) + r[1] + before(r[2])

    def fine_frame(which):
        t = spatial_taps(which)
        planes = []
        for p in range(2):
            if p == 0:
                r = [t[kw] + t[3 + kw] + above(t[6 + kw]) for kw in range(3)]
            else:
                r = [below(t[kw]) + t[3 + kw] + t[6 + kw] for kw in range(3)]
            planes.append(r[0] + r[1] + before(r[2]))
            planes.append(after(r[0]) + r[1] + r[2])
        return planes

    gather_relay(0)

    rows_wait(0)
    pieces = [chunk_swap([got_c[8 * half + j].astype(jnp.float32) for j in range(8)], chunk[:8]) for half in range(2)]
    values_c = jnp.concatenate(
        [
            jnp.concatenate([pieces[half][2 * quarter + frame] for quarter in range(4)], axis=0)
            for frame in range(2)
            for half in range(2)
        ],
        axis=1,
    )
    here_vals_c[...] = values_c.astype(jnp.bfloat16)
    pass_send(0)
    frames_start(0, row_of((row_sum(values_c), row_sum(values_c * values_c)), diagonal))
    rows_send(1)
    got_f[row] = sent_f[pl.ds(pl.multiple_of(row * width, width), width), :]

    loads[7].wait()
    told(0)
    tell(1)
    gather_finish(0)
    gathered = cot[...].reshape(2 * n_rows * 16, cot.shape[3])
    nt = (((1,), (1,)), ((), ()))
    prod[...] = lax.dot_general(weights_c[...], gathered, nt, preferred_element_type=jnp.float32)
    conv_before = jnp.concatenate([coarse_frame(0), coarse_frame(1)], axis=1)
    halo_out_c[...] = conv_before.astype(halo_out_c.dtype)
    halo_send(0)
    conv_c = jnp.concatenate([coarse_frame(2), coarse_frame(3)], axis=1)
    picked = one_hot(wide)
    cot_c = lax.dot_general(picked, gathered, nt, preferred_element_type=jnp.float32)

    entries_c = 16 * 2 * n_frames * cells
    entries_f = 4 * entries_c

    def norm_of(moments, entries):
        mean = group_total(column_of(moments, diagonal, 0)) / entries
        square = group_total(column_of(moments, diagonal, 1)) / entries
        return mean, lax.rsqrt(square - mean * mean + EPSILON)

    def through(values, gain, bias, mean, inv):
        normed = (values - mean) * inv
        pre = gain * normed + bias
        squash = jax.nn.sigmoid(pre)
        return normed, squash * (1.0 + pre * (1.0 - squash))

    mean_c, inv_c = norm_of(frames_total(0), entries_c)
    normed_c, slope_c = through(values_c, gain_c, bias_c, mean_c, inv_c)

    def sums_of(conv, normed, slope, conv_before, normed_before, slope_before):
        now, then = conv * slope, conv_before * slope_before
        pairs = ((row_sum(now), row_sum(then)), (row_sum(now * normed), row_sum(then * normed_before)))
        return tuple(own + jnp.where(fr > 0, earlier, 0.0) for own, earlier in pairs)

    pass_wait(0)
    before_c = through(prev_vals_c[...].astype(jnp.float32), gain_c, bias_c, mean_c, inv_c)
    here_c = sums_of(conv_c, normed_c, slope_c, conv_before, *before_c)
    frames_start(1, row_of(here_c, diagonal))

    rows_wait(1)
    swapped = []
    for half in range(2):
        swapped.append(chunk_swap([got_f[8 * half + j].astype(jnp.float32) for j in range(8)], chunk))
    values_f = jnp.concatenate([swapped[half][c] for c in range(8) for half in range(2)], axis=1)
    here_vals_f[...] = values_f.astype(jnp.bfloat16)
    pass_send(1)
    frames_start(2, row_of((row_sum(values_f), row_sum(values_f * values_f)), diagonal))

    halo_wait(0)
    pre_grad_c = (conv_c + halo_in_c[...].astype(jnp.float32)) * slope_c
    totals_c = frames_total(1)
    one_c, two_c = column_of(totals_c, diagonal, 0), column_of(totals_c, diagonal, 1)

    def level(cot, normed, pre_grad, gain, inv, one, two, entries):
        group_one = group_total(gain * one) / entries
        group_two = group_total(gain * two) / entries
        return cot + inv * (gain * pre_grad - group_one - normed * group_two)

    level_c = level(cot_c, normed_c, pre_grad_c, gain_c, inv_c, one_c, two_c, entries_c)
    quarter = (level_c * 0.25).astype(jnp.bfloat16)
    quart[row] = quarter
    gather_start(1)
    gather_relay(1)
    mean_f, inv_f = norm_of(frames_total(2), entries_f)
    normed_f, slope_f = through(here_vals_f[...].astype(jnp.float32), gain_f, bias_f, mean_f, inv_f)
    pass_wait(1)
    before_f = through(prev_vals_f[...].astype(jnp.float32), gain_f, bias_f, mean_f, inv_f)
    gather_finish(1)

    loads[8].wait()
    prod[...] = jnp.dot(
        weights_f[...], quart[...].reshape(n_rows * width, 2 * cells), preferred_element_type=jnp.float32
    )
    conv_before = jnp.concatenate(fine_frame(0) + fine_frame(1), axis=1)
    halo_out_f[...] = conv_before.astype(halo_out_f.dtype)
    halo_send(1)
    conv_f = jnp.concatenate(fine_frame(2) + fine_frame(3), axis=1)
    here_f = sums_of(conv_f, normed_f, slope_f, conv_before, *before_f)

    cells_all = n_dp * 2 * n_frames * cells
    scale_c, scale_f = 1.0 / cells_all**0.5, 1.0 / (4 * cells_all) ** 0.5
    n_z, n_xy = 4 * n_dp, 4 * n_frames
    in_z, in_xy = 4 * dp + z, 4 * fr + y

    def z_copy(target, source):
        return pltpu.make_async_remote_copy(
            src_ref=par_z.at[in_z],
            dst_ref=par_z.at[source],
            send_sem=par_sem.at[0],
            recv_sem=par_sem.at[1],
            device_id={"dp": lax.div(target, 4), "rows": 4 * y + lax.rem(target, 4)},
            device_id_type=MESH,
        )

    def xy_copy(target, source):
        return pltpu.make_async_remote_copy(
            src_ref=par_xy.at[in_xy],
            dst_ref=par_xy.at[source],
            send_sem=par_sem.at[2],
            recv_sem=par_sem.at[3],
            device_id={"frames": lax.div(target, 4), "rows": 4 * lax.rem(target, 4) + z},
            device_id_type=MESH,
        )

    def each(count, body):
        def step(d, carry):
            body(d)
            return carry

        lax.fori_loop(1, count, step, 0)

    mine = (here_f[1] * scale_f, here_f[0] * scale_f, here_c[1] * scale_c, here_c[0] * scale_c)
    par_z[in_z] = row_of(mine, diagonal)
    told(1)
    each(n_z, lambda d: z_copy(lax.rem(in_z + d, n_z), in_z).start())

    frames_start(3, row_of(here_f, diagonal))
    halo_wait(1)
    pre_grad_f = (conv_f + halo_in_f[...].astype(jnp.float32)) * slope_f
    totals_f = frames_total(3)
    one_f, two_f = column_of(totals_f, diagonal, 0), column_of(totals_f, diagonal, 1)

    four = [quarter[:, frame * cells : (frame + 1) * cells].astype(jnp.float32) for frame in range(2)]
    cot_f = jnp.concatenate([four[c // 4] for c in range(8)], axis=1)
    level_f = level(cot_f, normed_f, pre_grad_f, gain_f, inv_f, one_f, two_f, entries_f)
    for half in range(2):
        planes = [level_f[:, c * cells + half * LANES : c * cells + (half + 1) * LANES] for c in range(8)]
        for j, block in enumerate(chunk_swap(planes, chunk)):
            grad_out[8 * half + j] = block.astype(jnp.bfloat16)
    rows_send(2)
    grad_in[row] = grad_out[row]

    gather_sent(0)
    gather_sent(1)
    for stage in range(2):
        rows_sent(stage)
    for stage in range(4):
        all_of(stats.at[stage, pl.ds(0, n_frames - 1)], send_frames.at[stage])

    @pl.when(fr > 0)
    def _():
        halo_copy(0).wait_send()
        halo_copy(1).wait_send()

    @pl.when(fr < n_frames - 1)
    def _():
        pass_on(0).wait_send()
        pass_on(1).wait_send()

    all_of(par_z.at[pl.ds(0, n_z - 1)], par_sem.at[1])
    for k in range(4):
        total = par_z[k]
        for j in range(1, n_dp):
            total = total + par_z[4 * j + k]
        par_xy[in_xy, k : k + 1] = total
    each(n_xy, lambda d: xy_copy(lax.rem(in_xy + d, n_xy), in_xy).start())

    rows_wait(2)
    back = grad_in[...].reshape(n_rows * width, LANES).astype(jnp.float32).T.astype(jnp.bfloat16)
    out[...] = jnp.dot(to_old, back, preferred_element_type=jnp.float32).astype(out.dtype)

    rows_sent(2)
    all_of(par_z.at[pl.ds(0, n_z - 1)], par_sem.at[0])
    all_of(par_xy.at[pl.ds(0, n_xy - 1)], par_sem.at[3])
    sums = []
    for k in range(4):
        total = par_xy[k]
        for j in range(1, n_frames):
            total = total + par_xy[4 * j + k]
        sums.append(total)
    lines = [jnp.concatenate([sums[k][j : j + 1] for k in range(4)], axis=0) for j in range(4)]
    part = iota(lines[0].shape, 1) >> 5
    for bit in range(2):
        step = 1 << bit
        low = ((part >> bit) & 1) == 0
        for i in range(4):
            if i & step:
                continue
            one, two = lines[i], lines[i + step]
            lines[i] = jnp.where(low, one, pltpu.roll(two, 32 * step, 1))
            lines[i + step] = jnp.where(low, pltpu.roll(one, LANES - 32 * step, 1), two)
    for k in range(4):
        par[k] = lines[k]

    all_of(par_xy.at[pl.ds(0, n_xy - 1)], par_sem.at[2])


def finish(grad, par, out, *vectors):
    out[...] = grad[...]
    for k, vector in enumerate(vectors):
        vector[...] = par[k]


def shards(
    sizes,
    acts_fine,
    acts_coarse,
    grad_coarse,
    gain_fine,
    bias_fine,
    kernel_fine,
    gain_coarse,
    bias_coarse,
    kernel_coarse,
):
    n_dp, n_frames, n_rows = sizes
    channels = acts_fine.shape[-1]
    width = channels // n_rows
    positions = 2 * n_rows * 16
    bf16, f32 = jnp.bfloat16, jnp.float32
    vmem = pl.BlockSpec(memory_space=pltpu.VMEM)
    anywhere = pl.BlockSpec(memory_space=pl.ANY)
    dma = pltpu.SemaphoreType.DMA
    taps = kernel_fine.shape[0]
    held = (pltpu.VMEM((LANES, channels), bf16), pltpu.VMEM((4, channels // LANES, LANES), f32))
    out, par = pl.pallas_call(
        functools.partial(kernel, sizes),
        out_shape=held,
        in_specs=[anywhere] * 9,
        out_specs=(vmem, vmem),
        scratch_shapes=[
            pltpu.VMEM((LANES, channels), bf16),
            pltpu.VMEM((32, channels), bf16),
            pltpu.VMEM((4, 1, channels), f32),
            pltpu.VMEM((taps * width, channels), bf16),
            pltpu.VMEM((taps * width, channels), bf16),
            pltpu.VMEM((channels, LANES), bf16),
            pltpu.VMEM((n_rows, 8, LANES), bf16),
            pltpu.VMEM((n_rows, width, LANES), bf16),
            pltpu.VMEM((n_rows, 8, LANES), bf16),
            pltpu.VMEM((2, n_rows, 16, channels), bf16),
            pltpu.VMEM((n_rows, width, positions), bf16),
            pltpu.VMEM((taps * width, positions), f32),
            pltpu.VMEM((width, positions), bf16),
            pltpu.VMEM((width, positions), bf16),
            pltpu.VMEM((width, 4 * positions), bf16),
            pltpu.VMEM((width, 4 * positions), bf16),
            pltpu.VMEM((width, positions), bf16),
            pltpu.VMEM((width, positions), bf16),
            pltpu.VMEM((width, 4 * positions), bf16),
            pltpu.VMEM((width, 4 * positions), bf16),
            pltpu.VMEM((4, n_frames, 1, LANES), f32),
            pltpu.VMEM((4 * n_dp, 1, LANES), f32),
            pltpu.VMEM((4 * n_frames, 4, LANES), f32),
            pltpu.VMEM((n_rows, width, LANES), bf16),
            pltpu.VMEM((n_rows, width, LANES), bf16),
            dma((6,)),
            dma((3,)),
            dma((3,)),
            dma((4,)),
            dma((4,)),
            dma((2,)),
            dma((2,)),
            dma((2, 2)),
            dma((4,)),
            dma((2,)),
            dma((2, 8)),
            pltpu.SemaphoreType.REGULAR((2,)),
        ],
        compiler_params=pltpu.CompilerParams(collective_id=0, has_side_effects=True),
        name="levels",
    )(
        acts_fine.reshape(LANES, channels),
        acts_coarse.reshape(32, channels),
        grad_coarse.reshape(2, 16, channels),
        gain_fine.reshape(1, channels),
        bias_fine.reshape(1, channels),
        gain_coarse.reshape(1, channels),
        bias_coarse.reshape(1, channels),
        kernel_fine.reshape(taps * width, channels),
        kernel_coarse.reshape(taps * width, channels),
    )
    vector = jax.ShapeDtypeStruct((channels // LANES, LANES), f32)
    grad, *vectors = pl.pallas_call(
        finish,
        out_shape=(jax.ShapeDtypeStruct((LANES, channels), bf16), vector, vector, vector, vector),
        in_specs=[vmem, vmem],
        out_specs=(vmem,) * 5,
        name="finish",
    )(*(pltpu.with_memory_space_constraint(x, pltpu.VMEM) for x in (out, par)))
    return (grad.reshape(acts_fine.shape), *(v.reshape(channels) for v in vectors))


def solution(mesh):
    sizes = (mesh.shape["dp"], mesh.shape["frames"], mesh.shape["rows"])
    tall = P("dp", "frames", "rows", None, None)
    in_specs = (tall, tall, tall, P(), P(), P(None, "rows", None), P(), P(), P(None, "rows", None))
    out_specs = (tall, P(), P(), P(), P())
    return jax.shard_map(
        functools.partial(shards, sizes), mesh=mesh, in_specs=in_specs, out_specs=out_specs, check_vma=False
    )
```

```python
import functools

import jax
import jax.numpy as jnp
from jax import lax
from jax.experimental import pallas as pl
from jax.experimental.pallas import tpu as pltpu
from jax.sharding import PartitionSpec as P

GROUPS = 32
EPSILON = 1e-06
MESH = pl.DeviceIdType.MESH
LANES = 128


def iota(shape, dim):
    return lax.broadcasted_iota(jnp.int32, shape, dim)


def one_hot(cond, dtype=jnp.bfloat16):
    return jnp.where(cond, 1.0, 0.0).astype(dtype)


def fine_position(new):
    frame, p, q, a, b = new >> 6, (new >> 5) & 1, (new >> 4) & 1, (new >> 3) & 1, new & 7
    return frame * 64 + (2 * a + p) * 16 + 2 * b + q


def chunk_swap(arrays, chunk):
    arrays = list(arrays)
    for bit in range(3):
        step = 1 << bit
        low = ((chunk >> bit) & 1) == 0
        for i in range(8):
            if i & step:
                continue
            one, two = arrays[i], arrays[i + step]
            arrays[i] = jnp.where(low, one, pltpu.roll(two, 16 * step, 1))
            arrays[i + step] = jnp.where(low, pltpu.roll(one, LANES - 16 * step, 1), two)
    return arrays


def group_total(column):
    per_group = column.shape[0] // 2
    split = column.reshape(2, per_group, 1)
    return jnp.broadcast_to(jnp.sum(split, axis=1, keepdims=True), split.shape).reshape(column.shape)


def row_of(columns, diagonal):
    spread = jnp.zeros(diagonal.shape, jnp.float32)
    for k, column in enumerate(columns):
        spread = jnp.where(diagonal == k, column, spread)
    return jnp.sum(spread, axis=0, keepdims=True)


def column_of(row, diagonal, k):
    return row_sum(jnp.where(diagonal == k, row, 0.0))


def row_sum(x):
    return jnp.sum(x, axis=1, keepdims=True)


def kernel(
    sizes,
    acts_fine_hbm,
    acts_coarse_hbm,
    grad_coarse_hbm,
    gain_fine_hbm,
    bias_fine_hbm,
    gain_coarse_hbm,
    bias_coarse_hbm,
    kernel_fine,
    kernel_coarse,
    out,
    par,
    acts_fine,
    acts_coarse,
    vectors,
    weights_f,
    weights_c,
    sent_f,
    sent_c,
    got_f,
    got_c,
    cot,
    quart,
    prod,
    halo_out_c,
    halo_in_c,
    halo_out_f,
    halo_in_f,
    here_vals_c,
    prev_vals_c,
    here_vals_f,
    prev_vals_f,
    stats,
    par_z,
    par_xy,
    grad_out,
    grad_in,
    load_sem,
    send_rows,
    recv_rows,
    send_frames,
    recv_frames,
    send_halo,
    recv_halo,
    pass_sem,
    par_sem,
    send_relay,
    recv_relay,
    ready,
):
    n_dp, n_frames, n_rows = sizes
    dp, fr, row = lax.axis_index("dp"), lax.axis_index("frames"), lax.axis_index("rows")
    width = weights_f.shape[0] // 27

    loads = [
        pltpu.make_async_copy(grad_coarse_hbm, cot.at[:, row], load_sem.at[0]),
        pltpu.make_async_copy(acts_coarse_hbm, acts_coarse, load_sem.at[1]),
        pltpu.make_async_copy(acts_fine_hbm, acts_fine, load_sem.at[2]),
        pltpu.make_async_copy(gain_fine_hbm, vectors.at[0], load_sem.at[3]),
        pltpu.make_async_copy(bias_fine_hbm, vectors.at[1], load_sem.at[3]),
        pltpu.make_async_copy(gain_coarse_hbm, vectors.at[2], load_sem.at[3]),
        pltpu.make_async_copy(bias_coarse_hbm, vectors.at[3], load_sem.at[3]),
        pltpu.make_async_copy(kernel_coarse, weights_c, load_sem.at[4]),
        pltpu.make_async_copy(kernel_fine, weights_f, load_sem.at[5]),
    ]
    loads[0].start()

    even = dp + 1 - 2 * lax.rem(dp, 2)
    near_dp = [even] + [lax.rem(core + step, n_dp) for core in (dp, even) for step in (2, n_dp - 2)]
    barrier = pltpu.get_barrier_semaphore()
    for axis, me, count in (("rows", row, n_rows), ("frames", fr, n_frames)):

        def greet(d, carry, axis=axis, me=me, count=count):
            pl.semaphore_signal(barrier, inc=1, device_id={axis: lax.rem(me + d, count)}, device_id_type=MESH)
            return carry

        lax.fori_loop(1, count, greet, 0)
    for peer in near_dp:
        pl.semaphore_signal(barrier, inc=1, device_id={"dp": peer}, device_id_type=MESH)

    for load in loads[1:]:
        load.start()

    loads[1].wait()
    place, source = iota((LANES, 32), 0), iota((LANES, 32), 1)
    placed = jnp.dot(one_hot((place & 31) == source), acts_coarse[...], preferred_element_type=jnp.float32)
    quads = placed.T.reshape(n_rows, 4, 8, LANES)
    quad = iota((n_rows, 8, LANES), 2) >> 5
    folded = jnp.where(quad == 0, quads[:, 0], 0.0)
    for k in range(1, 4):
        folded = jnp.where(quad == k, quads[:, k], folded)
    sent_c[...] = folded.astype(jnp.bfloat16)

    loads[0].wait()
    pl.semaphore_wait(barrier, (n_rows - 1) + (n_frames - 1) + len(near_dp))

    def tell(round_):
        for peer in near_dp:
            pl.semaphore_signal(ready.at[round_], inc=1, device_id={"dp": peer}, device_id_type=MESH)

    def told(round_):
        if near_dp:
            pl.semaphore_wait(ready.at[round_], len(near_dp))

    def all_of(ref, sem):
        pltpu.make_async_copy(ref, ref, sem).wait()

    def slices(ref, index):
        return ref.at[pl.ds(pl.multiple_of(index * width, width), width)]

    def rows_copy(stage, target, source):
        if stage == 0:
            src, dst = sent_c.at[target], got_c.at[source]
        elif stage == 1:
            src, dst = slices(sent_f, target), got_f.at[source]
        else:
            src, dst = grad_out.at[target], grad_in.at[source]
        return pltpu.make_async_remote_copy(
            src_ref=src,
            dst_ref=dst,
            send_sem=send_rows.at[stage],
            recv_sem=recv_rows.at[stage],
            device_id={"rows": target},
            device_id_type=MESH,
        )

    y, z = lax.div(row, 4), lax.rem(row, 4)
    z_mate = (z, z + 1 - 2 * lax.rem(z, 2), lax.rem(z + 2, 4), 3 - z)
    y_up, y_down, y_far = lax.rem(y + 1, 4), lax.rem(y + 3, 4), lax.rem(y + 2, 4)

    def at(y_of, z_of):
        return 4 * y_of + z_of

    def relay(stage, kind, slot, target):
        block = (cot.at[:, slot], quart.at[slot])[stage]
        return pltpu.make_async_remote_copy(
            src_ref=block,
            dst_ref=block,
            send_sem=send_relay.at[stage],
            recv_sem=recv_relay.at[stage, kind],
            device_id={"rows": target},
            device_id_type=MESH,
        )

    up, down, far = at(y_up, z), at(y_down, z), at(y_far, z)
    last = 3

    def gather_start(stage):
        for kind, target in ((0, at(y, z_mate[1])), (last, up), (last, down), (1, at(y, z_mate[2])), (2, at(y, z_mate[3])), (last, far)):
            relay(stage, kind, row, target).start()

    def gather_relay(stage):
        for j in (1, 2, 3):
            slot = at(y, z_mate[j])
            relay(stage, j - 1, slot, row).wait_recv()
            for target in (far, up, down):
                relay(stage, last, slot, target).start()

    def gather_finish(stage):
        all_of((cot.at[:, pl.ds(0, 12)], quart.at[pl.ds(0, 12)])[stage], recv_relay.at[stage, last])

    def gather_sent(stage):
        all_of((cot.at[:, pl.ds(0, 15)], quart.at[pl.ds(0, 15)])[stage], send_relay.at[stage])

    def rows_send(stage):
        def step(d, carry):
            rows_copy(stage, lax.rem(row + d, n_rows), row).start()
            return carry

        lax.fori_loop(1, n_rows, step, 0)

    def rows_refs(stage):
        return (got_c, got_f, grad_in)[stage].at[pl.ds(0, n_rows - 1)]

    def rows_wait(stage):
        all_of(rows_refs(stage), recv_rows.at[stage])

    def rows_sent(stage):
        all_of(rows_refs(stage), send_rows.at[stage])

    def frames_copy(stage, target, source):
        return pltpu.make_async_remote_copy(
            src_ref=stats.at[stage, fr],
            dst_ref=stats.at[stage, source],
            send_sem=send_frames.at[stage],
            recv_sem=recv_frames.at[stage],
            device_id={"frames": target},
            device_id_type=MESH,
        )

    def frames_start(stage, block):
        stats[stage, fr] = block

        def step(d, carry):
            frames_copy(stage, lax.rem(fr + d, n_frames), fr).start()
            return carry

        lax.fori_loop(1, n_frames, step, 0)

    def frames_total(stage):
        all_of(stats.at[stage, pl.ds(0, n_frames - 1)], recv_frames.at[stage])
        total = stats[stage, 0]
        for k in range(1, n_frames):
            total = total + stats[stage, k]
        return total

    def halo_copy(stage):
        src, dst = ((halo_out_c, halo_in_c), (halo_out_f, halo_in_f))[stage]
        return pltpu.make_async_remote_copy(
            src_ref=src,
            dst_ref=dst,
            send_sem=send_halo.at[stage],
            recv_sem=recv_halo.at[stage],
            device_id={"frames": lax.rem(fr + n_frames - 1, n_frames)},
            device_id_type=MESH,
        )

    def halo_send(stage):
        @pl.when(fr > 0)
        def _():
            halo_copy(stage).start()

    def halo_wait(stage):
        @pl.when(fr < n_frames - 1)
        def _():
            halo_copy(stage).wait_recv()

        @pl.when(fr == n_frames - 1)
        def _():
            into = (halo_in_c, halo_in_f)[stage]
            into[...] = jnp.zeros_like(into)

    gather_start(0)
    rows_send(0)
    got_c[row] = sent_c[row]
    tell(0)

    loads[2].wait()
    new, old = iota((LANES, LANES), 0), iota((LANES, LANES), 1)
    to_new = one_hot(old == fine_position(new))
    to_old = one_hot(new == fine_position(old))
    moved = jnp.dot(to_new, acts_fine[...], preferred_element_type=jnp.float32)
    sent_f[...] = moved.T.astype(jnp.bfloat16)
    all_of(vectors, load_sem.at[3])

    def pass_on(stage):
        here, there = ((here_vals_c, prev_vals_c), (here_vals_f, prev_vals_f))[stage]
        return pltpu.make_async_remote_copy(
            src_ref=here,
            dst_ref=there,
            send_sem=pass_sem.at[0, stage],
            recv_sem=pass_sem.at[1, stage],
            device_id={"frames": lax.rem(fr + 1, n_frames)},
            device_id_type=MESH,
        )

    def pass_send(stage):
        @pl.when(fr < n_frames - 1)
        def _():
            pass_on(stage).start()

    def pass_wait(stage):
        @pl.when(fr > 0)
        def _():
            pass_on(stage).wait_recv()

        @pl.when(fr == 0)
        def _():
            into = (prev_vals_c, prev_vals_f)[stage]
            into[...] = jnp.zeros_like(into)

    wide = iota((width, vectors.shape[2]), 1) == row * width + iota((width, vectors.shape[2]), 0)

    def column(vector):
        return row_sum(jnp.where(wide, vector, 0.0))

    gain_f, bias_f, gain_c, bias_c = (column(vectors[k]) for k in range(4))
    lane, channel = iota((width, LANES), 1), iota((width, LANES), 0)
    chunk = lane >> 4
    diagonal = jnp.where((lane & 31) == channel, lane >> 5, -1)

    cells = 256
    spot = iota((width, cells), 1)
    top, bottom = spot >= 8, spot < cells - 8
    left, right = (spot & 7) > 0, (spot & 7) < 7

    def above(x):
        return jnp.where(top, pltpu.roll(x, 8, 1), 0.0)

    def below(x):
        return jnp.where(bottom, pltpu.roll(x, cells - 8, 1), 0.0)

    def before(x):
        return jnp.where(left, pltpu.roll(x, 1, 1), 0.0)

    def after(x):
        return jnp.where(right, pltpu.roll(x, cells - 1, 1), 0.0)

    def product(depth, tap, frame):
        at = (depth * 9 + tap) * width
        return prod[at : at + width, frame * cells : (frame + 1) * cells]

    def spatial_taps(which):
        terms = (((0, 0),), ((1, 0), (0, 1)), ((2, 0), (1, 1)), ((2, 1),))[which]
        taps = []
        for tap in range(9):
            total = product(terms[0][0], tap, terms[0][1])
            for depth, frame in terms[1:]:
                total = total + product(depth, tap, frame)
            taps.append(total)
        return taps

    def coarse_frame(which):
        t = spatial_taps(which)
        r = [below(t[kw]) + t[3 + kw] + above(t[6 + kw]) for kw in range(3)]
        return after(r[0]) + r[1] + before(r[2])

    def fine_frame(which):
        t = spatial_taps(which)
        planes = []
        for p in range(2):
            if p == 0:
                r = [t[kw] + t[3 + kw] + above(t[6 + kw]) for kw in range(3)]
            else:
                r = [below(t[kw]) + t[3 + kw] + t[6 + kw] for kw in range(3)]
            planes.append(r[0] + r[1] + before(r[2]))
            planes.append(after(r[0]) + r[1] + r[2])
        return planes

    gather_relay(0)

    rows_wait(0)
    pieces = [chunk_swap([got_c[8 * half + j].astype(jnp.float32) for j in range(8)], chunk[:8]) for half in range(2)]
    values_c = jnp.concatenate(
        [
            jnp.concatenate([pieces[half][2 * quarter + frame] for quarter in range(4)], axis=0)
            for frame in range(2)
            for half in range(2)
        ],
        axis=1,
    )
    here_vals_c[...] = values_c.astype(jnp.bfloat16)
    pass_send(0)
    frames_start(0, row_of((row_sum(values_c), row_sum(values_c * values_c)), diagonal))
    rows_send(1)
    got_f[row] = sent_f[pl.ds(pl.multiple_of(row * width, width), width), :]

    loads[7].wait()
    told(0)
    tell(1)
    gather_finish(0)
    gathered = cot[...].reshape(2 * n_rows * 16, cot.shape[3])
    nt = (((1,), (1,)), ((), ()))
    prod[...] = lax.dot_general(weights_c[...], gathered, nt, preferred_element_type=jnp.float32)
    conv_before = jnp.concatenate([coarse_frame(0), coarse_frame(1)], axis=1)
    halo_out_c[...] = conv_before.astype(halo_out_c.dtype)
    halo_send(0)
    conv_c = jnp.concatenate([coarse_frame(2), coarse_frame(3)], axis=1)
    picked = one_hot(wide)
    cot_c = lax.dot_general(picked, gathered, nt, preferred_element_type=jnp.float32)

    entries_c = 16 * 2 * n_frames * cells
    entries_f = 4 * entries_c

    def norm_of(moments, entries):
        mean = group_total(column_of(moments, diagonal, 0)) / entries
        square = group_total(column_of(moments, diagonal, 1)) / entries
        return mean, lax.rsqrt(square - mean * mean + EPSILON)

    def through(values, gain, bias, mean, inv):
        normed = (values - mean) * inv
        pre = gain * normed + bias
        squash = jax.nn.sigmoid(pre)
        return normed, squash * (1.0 + pre * (1.0 - squash))

    mean_c, inv_c = norm_of(frames_total(0), entries_c)
    normed_c, slope_c = through(values_c, gain_c, bias_c, mean_c, inv_c)

    def sums_of(conv, normed, slope, conv_before, normed_before, slope_before):
        now, then = conv * slope, conv_before * slope_before
        pairs = ((row_sum(now), row_sum(then)), (row_sum(now * normed), row_sum(then * normed_before)))
        return tuple(own + jnp.where(fr > 0, earlier, 0.0) for own, earlier in pairs)

    pass_wait(0)
    before_c = through(prev_vals_c[...].astype(jnp.float32), gain_c, bias_c, mean_c, inv_c)
    here_c = sums_of(conv_c, normed_c, slope_c, conv_before, *before_c)
    frames_start(1, row_of(here_c, diagonal))

    rows_wait(1)
    swapped = []
    for half in range(2):
        swapped.append(chunk_swap([got_f[8 * half + j].astype(jnp.float32) for j in range(8)], chunk))
    values_f = jnp.concatenate([swapped[half][c] for c in range(8) for half in range(2)], axis=1)
    here_vals_f[...] = values_f.astype(jnp.bfloat16)
    pass_send(1)
    frames_start(2, row_of((row_sum(values_f), row_sum(values_f * values_f)), diagonal))

    halo_wait(0)
    pre_grad_c = (conv_c + halo_in_c[...].astype(jnp.float32)) * slope_c
    totals_c = frames_total(1)
    one_c, two_c = column_of(totals_c, diagonal, 0), column_of(totals_c, diagonal, 1)

    def level(cot, normed, pre_grad, gain, inv, one, two, entries):
        group_one = group_total(gain * one) / entries
        group_two = group_total(gain * two) / entries
        return cot + inv * (gain * pre_grad - group_one - normed * group_two)

    level_c = level(cot_c, normed_c, pre_grad_c, gain_c, inv_c, one_c, two_c, entries_c)
    quarter = (level_c * 0.25).astype(jnp.bfloat16)
    quart[row] = quarter
    gather_start(1)
    gather_relay(1)
    mean_f, inv_f = norm_of(frames_total(2), entries_f)
    normed_f, slope_f = through(here_vals_f[...].astype(jnp.float32), gain_f, bias_f, mean_f, inv_f)
    pass_wait(1)
    before_f = through(prev_vals_f[...].astype(jnp.float32), gain_f, bias_f, mean_f, inv_f)
    gather_finish(1)

    loads[8].wait()
    prod[...] = jnp.dot(
        weights_f[...], quart[...].reshape(n_rows * width, 2 * cells), preferred_element_type=jnp.float32
    )
    conv_before = jnp.concatenate(fine_frame(0) + fine_frame(1), axis=1)
    halo_out_f[...] = conv_before.astype(halo_out_f.dtype)
    halo_send(1)
    conv_f = jnp.concatenate(fine_frame(2) + fine_frame(3), axis=1)
    here_f = sums_of(conv_f, normed_f, slope_f, conv_before, *before_f)

    cells_all = n_dp * 2 * n_frames * cells
    scale_c, scale_f = 1.0 / cells_all**0.5, 1.0 / (4 * cells_all) ** 0.5
    n_z, n_xy = 4 * n_dp, 4 * n_frames
    in_z, in_xy = 4 * dp + z, 4 * fr + y

    def z_copy(target, source):
        return pltpu.make_async_remote_copy(
            src_ref=par_z.at[in_z],
            dst_ref=par_z.at[source],
            send_sem=par_sem.at[0],
            recv_sem=par_sem.at[1],
            device_id={"dp": lax.div(target, 4), "rows": 4 * y + lax.rem(target, 4)},
            device_id_type=MESH,
        )

    def xy_copy(target, source):
        return pltpu.make_async_remote_copy(
            src_ref=par_xy.at[in_xy],
            dst_ref=par_xy.at[source],
            send_sem=par_sem.at[2],
            recv_sem=par_sem.at[3],
            device_id={"frames": lax.div(target, 4), "rows": 4 * lax.rem(target, 4) + z},
            device_id_type=MESH,
        )

    def each(count, body):
        def step(d, carry):
            body(d)
            return carry

        lax.fori_loop(1, count, step, 0)

    mine = (here_f[1] * scale_f, here_f[0] * scale_f, here_c[1] * scale_c, here_c[0] * scale_c)
    par_z[in_z] = row_of(mine, diagonal)
    told(1)
    each(n_z, lambda d: z_copy(lax.rem(in_z + 1 + lax.rem(d + n_z // 2 - 2, n_z - 1), n_z), in_z).start())

    frames_start(3, row_of(here_f, diagonal))
    halo_wait(1)
    pre_grad_f = (conv_f + halo_in_f[...].astype(jnp.float32)) * slope_f
    totals_f = frames_total(3)
    one_f, two_f = column_of(totals_f, diagonal, 0), column_of(totals_f, diagonal, 1)

    four = [quarter[:, frame * cells : (frame + 1) * cells].astype(jnp.float32) for frame in range(2)]
    cot_f = jnp.concatenate([four[c // 4] for c in range(8)], axis=1)
    level_f = level(cot_f, normed_f, pre_grad_f, gain_f, inv_f, one_f, two_f, entries_f)
    for half in range(2):
        planes = [level_f[:, c * cells + half * LANES : c * cells + (half + 1) * LANES] for c in range(8)]
        for j, block in enumerate(chunk_swap(planes, chunk)):
            grad_out[8 * half + j] = block.astype(jnp.bfloat16)
    rows_send(2)
    grad_in[row] = grad_out[row]

    gather_sent(0)
    gather_sent(1)
    for stage in range(2):
        rows_sent(stage)
    for stage in range(4):
        all_of(stats.at[stage, pl.ds(0, n_frames - 1)], send_frames.at[stage])

    @pl.when(fr > 0)
    def _():
        halo_copy(0).wait_send()
        halo_copy(1).wait_send()

    @pl.when(fr < n_frames - 1)
    def _():
        pass_on(0).wait_send()
        pass_on(1).wait_send()

    all_of(par_z.at[pl.ds(0, n_z - 1)], par_sem.at[1])
    for k in range(4):
        total = par_z[k]
        for j in range(1, n_dp):
            total = total + par_z[4 * j + k]
        par_xy[in_xy, k : k + 1] = total
    each(n_xy, lambda d: xy_copy(lax.rem(in_xy + d, n_xy), in_xy).start())

    rows_wait(2)
    back = grad_in[...].reshape(n_rows * width, LANES).astype(jnp.float32).T.astype(jnp.bfloat16)
    out[...] = jnp.dot(to_old, back, preferred_element_type=jnp.float32).astype(out.dtype)

    rows_sent(2)
    all_of(par_z.at[pl.ds(0, n_z - 1)], par_sem.at[0])
    all_of(par_xy.at[pl.ds(0, n_xy - 1)], par_sem.at[3])
    sums = []
    for k in range(4):
        total = par_xy[k]
        for j in range(1, n_frames):
            total = total + par_xy[4 * j + k]
        sums.append(total)
    lines = [jnp.concatenate([sums[k][j : j + 1] for k in range(4)], axis=0) for j in range(4)]
    part = iota(lines[0].shape, 1) >> 5
    for bit in range(2):
        step = 1 << bit
        low = ((part >> bit) & 1) == 0
        for i in range(4):
            if i & step:
                continue
            one, two = lines[i], lines[i + step]
            lines[i] = jnp.where(low, one, pltpu.roll(two, 32 * step, 1))
            lines[i + step] = jnp.where(low, pltpu.roll(one, LANES - 32 * step, 1), two)
    for k in range(4):
        par[k] = lines[k]

    all_of(par_xy.at[pl.ds(0, n_xy - 1)], par_sem.at[2])


def finish(grad, par, out, *vectors):
    out[...] = grad[...]
    for k, vector in enumerate(vectors):
        vector[...] = par[k]


def shards(
    sizes,
    acts_fine,
    acts_coarse,
    grad_coarse,
    gain_fine,
    bias_fine,
    kernel_fine,
    gain_coarse,
    bias_coarse,
    kernel_coarse,
):
    n_dp, n_frames, n_rows = sizes
    channels = acts_fine.shape[-1]
    width = channels // n_rows
    positions = 2 * n_rows * 16
    bf16, f32 = jnp.bfloat16, jnp.float32
    vmem = pl.BlockSpec(memory_space=pltpu.VMEM)
    anywhere = pl.BlockSpec(memory_space=pl.ANY)
    dma = pltpu.SemaphoreType.DMA
    taps = kernel_fine.shape[0]
    held = (pltpu.VMEM((LANES, channels), bf16), pltpu.VMEM((4, channels // LANES, LANES), f32))
    out, par = pl.pallas_call(
        functools.partial(kernel, sizes),
        out_shape=held,
        in_specs=[anywhere] * 9,
        out_specs=(vmem, vmem),
        scratch_shapes=[
            pltpu.VMEM((LANES, channels), bf16),
            pltpu.VMEM((32, channels), bf16),
            pltpu.VMEM((4, 1, channels), f32),
            pltpu.VMEM((taps * width, channels), bf16),
            pltpu.VMEM((taps * width, channels), bf16),
            pltpu.VMEM((channels, LANES), bf16),
            pltpu.VMEM((n_rows, 8, LANES), bf16),
            pltpu.VMEM((n_rows, width, LANES), bf16),
            pltpu.VMEM((n_rows, 8, LANES), bf16),
            pltpu.VMEM((2, n_rows, 16, channels), bf16),
            pltpu.VMEM((n_rows, width, positions), bf16),
            pltpu.VMEM((taps * width, positions), f32),
            pltpu.VMEM((width, positions), bf16),
            pltpu.VMEM((width, positions), bf16),
            pltpu.VMEM((width, 4 * positions), bf16),
            pltpu.VMEM((width, 4 * positions), bf16),
            pltpu.VMEM((width, positions), bf16),
            pltpu.VMEM((width, positions), bf16),
            pltpu.VMEM((width, 4 * positions), bf16),
            pltpu.VMEM((width, 4 * positions), bf16),
            pltpu.VMEM((4, n_frames, 1, LANES), f32),
            pltpu.VMEM((4 * n_dp, 1, LANES), f32),
            pltpu.VMEM((4 * n_frames, 4, LANES), f32),
            pltpu.VMEM((n_rows, width, LANES), bf16),
            pltpu.VMEM((n_rows, width, LANES), bf16),
            dma((6,)),
            dma((3,)),
            dma((3,)),
            dma((4,)),
            dma((4,)),
            dma((2,)),
            dma((2,)),
            dma((2, 2)),
            dma((4,)),
            dma((2,)),
            dma((2, 4)),
            pltpu.SemaphoreType.REGULAR((2,)),
        ],
        compiler_params=pltpu.CompilerParams(collective_id=0, has_side_effects=True),
        name="levels",
    )(
        acts_fine.reshape(LANES, channels),
        acts_coarse.reshape(32, channels),
        grad_coarse.reshape(2, 16, channels),
        gain_fine.reshape(1, channels),
        bias_fine.reshape(1, channels),
        gain_coarse.reshape(1, channels),
        bias_coarse.reshape(1, channels),
        kernel_fine.reshape(taps * width, channels),
        kernel_coarse.reshape(taps * width, channels),
    )
    vector = jax.ShapeDtypeStruct((channels // LANES, LANES), f32)
    grad, *vectors = pl.pallas_call(
        finish,
        out_shape=(jax.ShapeDtypeStruct((LANES, channels), bf16), vector, vector, vector, vector),
        in_specs=[vmem, vmem],
        out_specs=(vmem,) * 5,
        name="finish",
    )(*(pltpu.with_memory_space_constraint(x, pltpu.VMEM) for x in (out, par)))
    return (grad.reshape(acts_fine.shape), *(v.reshape(channels) for v in vectors))


def solution(mesh):
    sizes = (mesh.shape["dp"], mesh.shape["frames"], mesh.shape["rows"])
    tall = P("dp", "frames", "rows", None, None)
    in_specs = (tall, tall, tall, P(), P(), P(None, "rows", None), P(), P(), P(None, "rows", None))
    out_specs = (tall, P(), P(), P(), P())
    return jax.shard_map(
        functools.partial(shards, sizes), mesh=mesh, in_specs=in_specs, out_specs=out_specs, check_vma=False
    )
```

```python
import functools

import jax
import jax.numpy as jnp
from jax import lax
from jax.experimental import pallas as pl
from jax.experimental.pallas import tpu as pltpu
from jax.sharding import PartitionSpec as P

GROUPS = 32
EPSILON = 1e-06
MESH = pl.DeviceIdType.MESH
LANES = 128


def iota(shape, dim):
    return lax.broadcasted_iota(jnp.int32, shape, dim)


def one_hot(cond, dtype=jnp.bfloat16):
    return jnp.where(cond, 1.0, 0.0).astype(dtype)


def fine_position(new):
    frame, p, q, a, b = new >> 6, (new >> 5) & 1, (new >> 4) & 1, (new >> 3) & 1, new & 7
    return frame * 64 + (2 * a + p) * 16 + 2 * b + q


def chunk_swap(arrays, chunk):
    arrays = list(arrays)
    for bit in range(3):
        step = 1 << bit
        low = ((chunk >> bit) & 1) == 0
        for i in range(8):
            if i & step:
                continue
            one, two = arrays[i], arrays[i + step]
            arrays[i] = jnp.where(low, one, pltpu.roll(two, 16 * step, 1))
            arrays[i + step] = jnp.where(low, pltpu.roll(one, LANES - 16 * step, 1), two)
    return arrays


def group_total(column):
    per_group = column.shape[0] // 2
    split = column.reshape(2, per_group, 1)
    return jnp.broadcast_to(jnp.sum(split, axis=1, keepdims=True), split.shape).reshape(column.shape)


def row_of(columns, diagonal):
    spread = jnp.zeros(diagonal.shape, jnp.float32)
    for k, column in enumerate(columns):
        spread = jnp.where(diagonal == k, column, spread)
    return jnp.sum(spread, axis=0, keepdims=True)


def column_of(row, diagonal, k):
    return row_sum(jnp.where(diagonal == k, row, 0.0))


def row_sum(x):
    return jnp.sum(x, axis=1, keepdims=True)


def kernel(
    sizes,
    acts_fine_hbm,
    acts_coarse_hbm,
    grad_coarse_hbm,
    gain_fine_hbm,
    bias_fine_hbm,
    gain_coarse_hbm,
    bias_coarse_hbm,
    kernel_fine,
    kernel_coarse,
    out,
    par,
    acts_fine,
    acts_coarse,
    vectors,
    weights_f,
    weights_c,
    sent_f,
    sent_c,
    got_f,
    got_c,
    cot,
    quart,
    prod_0,
    prod_1,
    prod_2,
    halo_out_c,
    halo_in_c,
    halo_out_f,
    halo_in_f,
    here_vals_c,
    prev_vals_c,
    here_vals_f,
    prev_vals_f,
    stats,
    par_z,
    par_xy,
    grad_out,
    grad_in,
    load_sem,
    send_rows,
    recv_rows,
    send_frames,
    recv_frames,
    send_halo,
    recv_halo,
    pass_sem,
    par_sem,
    send_relay,
    recv_relay,
    ready,
):
    n_dp, n_frames, n_rows = sizes
    prods = (prod_0, prod_1, prod_2)
    dp, fr, row = lax.axis_index("dp"), lax.axis_index("frames"), lax.axis_index("rows")
    width = weights_f.shape[0] // 27

    loads = [
        pltpu.make_async_copy(grad_coarse_hbm, cot.at[:, row], load_sem.at[0]),
        pltpu.make_async_copy(acts_coarse_hbm, acts_coarse, load_sem.at[1]),
        pltpu.make_async_copy(acts_fine_hbm, acts_fine, load_sem.at[2]),
        pltpu.make_async_copy(gain_fine_hbm, vectors.at[0], load_sem.at[3]),
        pltpu.make_async_copy(bias_fine_hbm, vectors.at[1], load_sem.at[3]),
        pltpu.make_async_copy(gain_coarse_hbm, vectors.at[2], load_sem.at[3]),
        pltpu.make_async_copy(bias_coarse_hbm, vectors.at[3], load_sem.at[3]),
        pltpu.make_async_copy(kernel_coarse, weights_c, load_sem.at[4]),
        pltpu.make_async_copy(kernel_fine, weights_f, load_sem.at[5]),
    ]
    loads[0].start()

    even = dp + 1 - 2 * lax.rem(dp, 2)
    near_dp = [even] + [lax.rem(core + step, n_dp) for core in (dp, even) for step in (2, n_dp - 2)]
    y, z = lax.div(row, 4), lax.rem(row, 4)
    z_mate = (z, z + 1 - 2 * lax.rem(z, 2), lax.rem(z + 2, 4), 3 - z)
    y_up, y_down, y_far = lax.rem(y + 1, 4), lax.rem(y + 3, 4), lax.rem(y + 2, 4)
    greeted = [{"rows": 4 * y_far + z_of} for z_of in z_mate] + [{"dp": peer} for peer in near_dp]
    greeted += [{"rows": 4 * y_of + z_of} for y_of in (y_up, y_down) for z_of in z_mate]
    greeted += [{"rows": 4 * y + z_of} for z_of in z_mate[1:]]
    greeted += [{"frames": lax.rem(fr + step, n_frames)} for step in range(1, n_frames)]
    barrier = pltpu.get_barrier_semaphore()
    for peer in greeted:
        pl.semaphore_signal(barrier, inc=1, device_id=peer, device_id_type=MESH)

    for load in loads[1:]:
        load.start()

    loads[1].wait()
    place, source = iota((LANES, 32), 0), iota((LANES, 32), 1)
    placed = jnp.dot(one_hot((place & 31) == source), acts_coarse[...], preferred_element_type=jnp.float32)
    quads = placed.T.reshape(n_rows, 4, 8, LANES)
    quad = iota((n_rows, 8, LANES), 2) >> 5
    folded = jnp.where(quad == 0, quads[:, 0], 0.0)
    for k in range(1, 4):
        folded = jnp.where(quad == k, quads[:, k], folded)
    sent_c[...] = folded.astype(jnp.bfloat16)

    loads[0].wait()
    pl.semaphore_wait(barrier, len(greeted))

    def tell(round_):
        for peer in near_dp:
            pl.semaphore_signal(ready.at[round_], inc=1, device_id={"dp": peer}, device_id_type=MESH)

    def told(round_):
        if near_dp:
            pl.semaphore_wait(ready.at[round_], len(near_dp))

    def all_of(ref, sem):
        pltpu.make_async_copy(ref, ref, sem).wait()

    def slices(ref, index):
        return ref.at[pl.ds(pl.multiple_of(index * width, width), width)]

    def rows_copy(stage, target, source):
        if stage == 0:
            src, dst = sent_c.at[target], got_c.at[source]
        elif stage == 1:
            src, dst = slices(sent_f, target), got_f.at[source]
        else:
            src, dst = grad_out.at[target], grad_in.at[source]
        return pltpu.make_async_remote_copy(
            src_ref=src,
            dst_ref=dst,
            send_sem=send_rows.at[stage],
            recv_sem=recv_rows.at[stage],
            device_id={"rows": target},
            device_id_type=MESH,
        )

    def at(y_of, z_of):
        return 4 * y_of + z_of

    def relay(stage, kind, slot, target):
        block = (cot.at[:, slot], quart.at[slot])[stage]
        return pltpu.make_async_remote_copy(
            src_ref=block,
            dst_ref=block,
            send_sem=send_relay.at[stage],
            recv_sem=recv_relay.at[stage, kind],
            device_id={"rows": target},
            device_id_type=MESH,
        )

    up, down, far = at(y_up, z), at(y_down, z), at(y_far, z)
    last = 3

    def gather_start(stage):
        for kind, target in ((0, at(y, z_mate[1])), (last, up), (last, down), (1, at(y, z_mate[2])), (2, at(y, z_mate[3])), (last, far)):
            relay(stage, kind, row, target).start()

    def gather_relay(stage):
        for j in (1, 2, 3):
            slot = at(y, z_mate[j])
            relay(stage, j - 1, slot, row).wait_recv()
            for target in (far, up, down):
                relay(stage, last, slot, target).start()

    def gather_finish(stage):
        all_of((cot.at[:, pl.ds(0, 12)], quart.at[pl.ds(0, 12)])[stage], recv_relay.at[stage, last])

    def gather_sent(stage):
        all_of((cot.at[:, pl.ds(0, 15)], quart.at[pl.ds(0, 15)])[stage], send_relay.at[stage])

    def rows_send(stage):
        def step(d, carry):
            rows_copy(stage, lax.rem(row + d, n_rows), row).start()
            return carry

        lax.fori_loop(1, n_rows, step, 0)

    def rows_refs(stage):
        return (got_c, got_f, grad_in)[stage].at[pl.ds(0, n_rows - 1)]

    def rows_wait(stage):
        all_of(rows_refs(stage), recv_rows.at[stage])

    def rows_sent(stage):
        all_of(rows_refs(stage), send_rows.at[stage])

    def frames_copy(stage, target, source):
        return pltpu.make_async_remote_copy(
            src_ref=stats.at[stage, fr],
            dst_ref=stats.at[stage, source],
            send_sem=send_frames.at[stage],
            recv_sem=recv_frames.at[stage],
            device_id={"frames": target},
            device_id_type=MESH,
        )

    def frames_start(stage, block):
        stats[stage, fr] = block

        def step(d, carry):
            frames_copy(stage, lax.rem(fr + d, n_frames), fr).start()
            return carry

        lax.fori_loop(1, n_frames, step, 0)

    def frames_total(stage):
        all_of(stats.at[stage, pl.ds(0, n_frames - 1)], recv_frames.at[stage])
        total = stats[stage, 0]
        for k in range(1, n_frames):
            total = total + stats[stage, k]
        return total

    def halo_copy(stage):
        src, dst = ((halo_out_c, halo_in_c), (halo_out_f, halo_in_f))[stage]
        return pltpu.make_async_remote_copy(
            src_ref=src,
            dst_ref=dst,
            send_sem=send_halo.at[stage],
            recv_sem=recv_halo.at[stage],
            device_id={"frames": lax.rem(fr + n_frames - 1, n_frames)},
            device_id_type=MESH,
        )

    def halo_send(stage):
        @pl.when(fr > 0)
        def _():
            halo_copy(stage).start()

    def halo_wait(stage):
        @pl.when(fr < n_frames - 1)
        def _():
            halo_copy(stage).wait_recv()

        @pl.when(fr == n_frames - 1)
        def _():
            into = (halo_in_c, halo_in_f)[stage]
            into[...] = jnp.zeros_like(into)

    gather_start(0)
    rows_send(0)
    got_c[row] = sent_c[row]
    tell(0)

    loads[2].wait()
    new, old = iota((LANES, LANES), 0), iota((LANES, LANES), 1)
    to_new = one_hot(old == fine_position(new))
    to_old = one_hot(new == fine_position(old))
    moved = jnp.dot(to_new, acts_fine[...], preferred_element_type=jnp.float32)
    sent_f[...] = moved.T.astype(jnp.bfloat16)
    all_of(vectors, load_sem.at[3])

    def pass_on(stage):
        here, there = ((here_vals_c, prev_vals_c), (here_vals_f, prev_vals_f))[stage]
        return pltpu.make_async_remote_copy(
            src_ref=here,
            dst_ref=there,
            send_sem=pass_sem.at[0, stage],
            recv_sem=pass_sem.at[1, stage],
            device_id={"frames": lax.rem(fr + 1, n_frames)},
            device_id_type=MESH,
        )

    def pass_send(stage):
        @pl.when(fr < n_frames - 1)
        def _():
            pass_on(stage).start()

    def pass_wait(stage):
        @pl.when(fr > 0)
        def _():
            pass_on(stage).wait_recv()

        @pl.when(fr == 0)
        def _():
            into = (prev_vals_c, prev_vals_f)[stage]
            into[...] = jnp.zeros_like(into)

    wide = iota((width, vectors.shape[2]), 1) == row * width + iota((width, vectors.shape[2]), 0)

    def column(vector):
        return row_sum(jnp.where(wide, vector, 0.0))

    gain_f, bias_f, gain_c, bias_c = (column(vectors[k]) for k in range(4))
    lane, channel = iota((width, LANES), 1), iota((width, LANES), 0)
    chunk = lane >> 4
    diagonal = jnp.where((lane & 31) == channel, lane >> 5, -1)

    cells = 256
    spot = iota((width, cells), 1)
    top, bottom = spot >= 8, spot < cells - 8
    left, right = (spot & 7) > 0, (spot & 7) < 7

    def above(x):
        return jnp.where(top, pltpu.roll(x, 8, 1), 0.0)

    def below(x):
        return jnp.where(bottom, pltpu.roll(x, cells - 8, 1), 0.0)

    def before(x):
        return jnp.where(left, pltpu.roll(x, 1, 1), 0.0)

    def after(x):
        return jnp.where(right, pltpu.roll(x, cells - 1, 1), 0.0)

    def product(depth, tap, frame):
        return prods[depth][tap * width : (tap + 1) * width, frame * cells : (frame + 1) * cells]

    def spatial_taps(which):
        terms = (((0, 0),), ((1, 0), (0, 1)), ((2, 0), (1, 1)), ((2, 1),))[which]
        taps = []
        for tap in range(9):
            total = product(terms[0][0], tap, terms[0][1])
            for depth, frame in terms[1:]:
                total = total + product(depth, tap, frame)
            taps.append(total)
        return taps

    def coarse_frame(which):
        t = spatial_taps(which)
        r = [below(t[kw]) + t[3 + kw] + above(t[6 + kw]) for kw in range(3)]
        return after(r[0]) + r[1] + before(r[2])

    def fine_frame(which):
        t = spatial_taps(which)
        planes = []
        for p in range(2):
            if p == 0:
                r = [t[kw] + t[3 + kw] + above(t[6 + kw]) for kw in range(3)]
            else:
                r = [below(t[kw]) + t[3 + kw] + t[6 + kw] for kw in range(3)]
            planes.append(r[0] + r[1] + before(r[2]))
            planes.append(after(r[0]) + r[1] + r[2])
        return planes

    gather_relay(0)

    rows_wait(0)
    pieces = [chunk_swap([got_c[8 * half + j].astype(jnp.float32) for j in range(8)], chunk[:8]) for half in range(2)]
    values_c = jnp.concatenate(
        [
            jnp.concatenate([pieces[half][2 * quarter + frame] for quarter in range(4)], axis=0)
            for frame in range(2)
            for half in range(2)
        ],
        axis=1,
    )
    here_vals_c[...] = values_c.astype(jnp.bfloat16)
    frames_start(0, row_of((row_sum(values_c), row_sum(values_c * values_c)), diagonal))
    pass_send(0)
    rows_send(1)
    got_f[row] = sent_f[pl.ds(pl.multiple_of(row * width, width), width), :]

    loads[7].wait()
    told(0)
    tell(1)
    gather_finish(0)
    gathered = cot[...].reshape(2 * n_rows * 16, cot.shape[3])
    nt = (((1,), (1,)), ((), ()))

    def depth_c(depth):
        at = depth * 9 * width
        prods[depth][...] = lax.dot_general(
            weights_c[at : at + 9 * width, :], gathered, nt, preferred_element_type=jnp.float32
        )

    depth_c(0)
    first = coarse_frame(0)
    depth_c(1)
    second = coarse_frame(1)
    conv_before = jnp.concatenate([first, second], axis=1)
    halo_out_c[...] = conv_before.astype(halo_out_c.dtype)
    depth_c(2)
    conv_c = jnp.concatenate([coarse_frame(2), coarse_frame(3)], axis=1)
    picked = one_hot(wide)
    cot_c = lax.dot_general(picked, gathered, nt, preferred_element_type=jnp.float32)

    entries_c = 16 * 2 * n_frames * cells
    entries_f = 4 * entries_c

    def norm_of(moments, entries):
        mean = group_total(column_of(moments, diagonal, 0)) / entries
        square = group_total(column_of(moments, diagonal, 1)) / entries
        return mean, lax.rsqrt(square - mean * mean + EPSILON)

    def through(values, gain, bias, mean, inv):
        normed = (values - mean) * inv
        pre = gain * normed + bias
        squash = jax.nn.sigmoid(pre)
        return normed, squash * (1.0 + pre * (1.0 - squash))

    mean_c, inv_c = norm_of(frames_total(0), entries_c)
    normed_c, slope_c = through(values_c, gain_c, bias_c, mean_c, inv_c)

    def sums_of(conv, normed, slope, conv_before, normed_before, slope_before):
        now, then = conv * slope, conv_before * slope_before
        pairs = ((row_sum(now), row_sum(then)), (row_sum(now * normed), row_sum(then * normed_before)))
        return tuple(own + jnp.where(fr > 0, earlier, 0.0) for own, earlier in pairs)

    pass_wait(0)
    before_c = through(prev_vals_c[...].astype(jnp.float32), gain_c, bias_c, mean_c, inv_c)
    here_c = sums_of(conv_c, normed_c, slope_c, conv_before, *before_c)
    frames_start(1, row_of(here_c, diagonal))
    halo_send(0)

    rows_wait(1)
    swapped = []
    for half in range(2):
        swapped.append(chunk_swap([got_f[8 * half + j].astype(jnp.float32) for j in range(8)], chunk))
    values_f = jnp.concatenate([swapped[half][c] for c in range(8) for half in range(2)], axis=1)
    here_vals_f[...] = values_f.astype(jnp.bfloat16)
    frames_start(2, row_of((row_sum(values_f), row_sum(values_f * values_f)), diagonal))
    pass_send(1)

    halo_wait(0)
    pre_grad_c = (conv_c + halo_in_c[...].astype(jnp.float32)) * slope_c
    base_c, lean_c = cot_c + inv_c * (gain_c * pre_grad_c), inv_c * normed_c
    totals_c = frames_total(1)
    one_c, two_c = column_of(totals_c, diagonal, 0), column_of(totals_c, diagonal, 1)

    def level(base, slope, gain, inv, one, two, entries):
        group_one = group_total(gain * one) / entries
        group_two = group_total(gain * two) / entries
        return base - inv * group_one - slope * group_two

    level_c = level(base_c, lean_c, gain_c, inv_c, one_c, two_c, entries_c)
    quarter = (level_c * 0.25).astype(jnp.bfloat16)
    quart[row] = quarter
    gather_start(1)
    gather_relay(1)
    mean_f, inv_f = norm_of(frames_total(2), entries_f)
    normed_f, slope_f = through(here_vals_f[...].astype(jnp.float32), gain_f, bias_f, mean_f, inv_f)
    pass_wait(1)
    before_f = through(prev_vals_f[...].astype(jnp.float32), gain_f, bias_f, mean_f, inv_f)
    gather_finish(1)

    loads[8].wait()
    quarters = quart[...].reshape(n_rows * width, 2 * cells)

    def depth_f(depth):
        at = depth * 9 * width
        prods[depth][...] = jnp.dot(
            weights_f[at : at + 9 * width, :], quarters, preferred_element_type=jnp.float32
        )

    depth_f(0)
    first = fine_frame(0)
    depth_f(1)
    second = fine_frame(1)
    conv_before = jnp.concatenate(first + second, axis=1)
    halo_out_f[...] = conv_before.astype(halo_out_f.dtype)
    halo_send(1)
    depth_f(2)
    conv_f = jnp.concatenate(fine_frame(2) + fine_frame(3), axis=1)
    here_f = sums_of(conv_f, normed_f, slope_f, conv_before, *before_f)

    cells_all = n_dp * 2 * n_frames * cells
    scale_c, scale_f = 1.0 / cells_all**0.5, 1.0 / (4 * cells_all) ** 0.5
    n_z, n_xy = 4 * n_dp, 4 * n_frames
    in_z, in_xy = 4 * dp + z, 4 * fr + y

    def z_copy(dp_of, z_of):
        return pltpu.make_async_remote_copy(
            src_ref=par_z.at[in_z],
            dst_ref=par_z.at[in_z],
            send_sem=par_sem.at[0],
            recv_sem=par_sem.at[1],
            device_id={"dp": dp_of, "rows": 4 * y + z_of},
            device_id_type=MESH,
        )

    def xy_copy(fr_of, y_of):
        return pltpu.make_async_remote_copy(
            src_ref=par_xy.at[in_xy],
            dst_ref=par_xy.at[in_xy],
            send_sem=par_sem.at[2],
            recv_sem=par_sem.at[3],
            device_id={"frames": fr_of, "rows": 4 * y_of + z},
            device_id_type=MESH,
        )

    mine = (here_f[1] * scale_f, here_f[0] * scale_f, here_c[1] * scale_c, here_c[0] * scale_c)
    par_z[in_z] = row_of(mine, diagonal)
    told(1)
    for step in (4, 5, 3, 6, 2, 7, 1):
        there = lax.rem(dp + step, n_dp)
        for k in range(4):
            z_copy(there, k).start()
    for k in (1, 2, 3):
        z_copy(dp, z_mate[k]).start()
    frames_start(3, row_of(here_f, diagonal))
    halo_wait(1)
    pre_grad_f = (conv_f + halo_in_f[...].astype(jnp.float32)) * slope_f
    four = [quarter[:, frame * cells : (frame + 1) * cells].astype(jnp.float32) for frame in range(2)]
    cot_f = jnp.concatenate([four[c // 4] for c in range(8)], axis=1)
    base_f, lean_f = cot_f + inv_f * (gain_f * pre_grad_f), inv_f * normed_f
    totals_f = frames_total(3)
    one_f, two_f = column_of(totals_f, diagonal, 0), column_of(totals_f, diagonal, 1)

    level_f = level(base_f, lean_f, gain_f, inv_f, one_f, two_f, entries_f)
    for half in range(2):
        planes = [level_f[:, c * cells + half * LANES : c * cells + (half + 1) * LANES] for c in range(8)]
        for j, block in enumerate(chunk_swap(planes, chunk)):
            grad_out[8 * half + j] = block.astype(jnp.bfloat16)
    rows_send(2)
    grad_in[row] = grad_out[row]

    gather_sent(0)
    gather_sent(1)
    for stage in range(2):
        rows_sent(stage)
    for stage in range(4):
        all_of(stats.at[stage, pl.ds(0, n_frames - 1)], send_frames.at[stage])

    @pl.when(fr > 0)
    def _():
        halo_copy(0).wait_send()
        halo_copy(1).wait_send()

    @pl.when(fr < n_frames - 1)
    def _():
        pass_on(0).wait_send()
        pass_on(1).wait_send()

    all_of(par_z.at[pl.ds(0, n_z - 1)], par_sem.at[1])
    for k in range(4):
        total = par_z[k]
        for j in range(1, n_dp):
            total = total + par_z[4 * j + k]
        par_xy[in_xy, k : k + 1] = total
    for step in (2, 1, 3):
        there = lax.rem(fr + step, n_frames)
        for k in range(4):
            xy_copy(there, k).start()
    for k in (y_far, y_up, y_down):
        xy_copy(fr, k).start()

    rows_wait(2)
    back = grad_in[...].reshape(n_rows * width, LANES).astype(jnp.float32).T.astype(jnp.bfloat16)
    out[...] = jnp.dot(to_old, back, preferred_element_type=jnp.float32).astype(out.dtype)

    rows_sent(2)
    all_of(par_z.at[pl.ds(0, n_z - 1)], par_sem.at[0])
    all_of(par_xy.at[pl.ds(0, n_xy - 1)], par_sem.at[3])
    sums = []
    for k in range(4):
        total = par_xy[k]
        for j in range(1, n_frames):
            total = total + par_xy[4 * j + k]
        sums.append(total)
    lines = [jnp.concatenate([sums[k][j : j + 1] for k in range(4)], axis=0) for j in range(4)]
    part = iota(lines[0].shape, 1) >> 5
    for bit in range(2):
        step = 1 << bit
        low = ((part >> bit) & 1) == 0
        for i in range(4):
            if i & step:
                continue
            one, two = lines[i], lines[i + step]
            lines[i] = jnp.where(low, one, pltpu.roll(two, 32 * step, 1))
            lines[i + step] = jnp.where(low, pltpu.roll(one, LANES - 32 * step, 1), two)
    for k in range(4):
        par[k] = lines[k]

    all_of(par_xy.at[pl.ds(0, n_xy - 1)], par_sem.at[2])


def finish(grad, par, out, *vectors):
    out[...] = grad[...]
    for k, vector in enumerate(vectors):
        vector[...] = par[k]


def shards(
    sizes,
    acts_fine,
    acts_coarse,
    grad_coarse,
    gain_fine,
    bias_fine,
    kernel_fine,
    gain_coarse,
    bias_coarse,
    kernel_coarse,
):
    n_dp, n_frames, n_rows = sizes
    channels = acts_fine.shape[-1]
    width = channels // n_rows
    positions = 2 * n_rows * 16
    bf16, f32 = jnp.bfloat16, jnp.float32
    vmem = pl.BlockSpec(memory_space=pltpu.VMEM)
    anywhere = pl.BlockSpec(memory_space=pl.ANY)
    dma = pltpu.SemaphoreType.DMA
    taps = kernel_fine.shape[0]
    held = (pltpu.VMEM((LANES, channels), bf16), pltpu.VMEM((4, channels // LANES, LANES), f32))
    out, par = pl.pallas_call(
        functools.partial(kernel, sizes),
        out_shape=held,
        in_specs=[anywhere] * 9,
        out_specs=(vmem, vmem),
        scratch_shapes=[
            pltpu.VMEM((LANES, channels), bf16),
            pltpu.VMEM((32, channels), bf16),
            pltpu.VMEM((4, 1, channels), f32),
            pltpu.VMEM((taps * width, channels), bf16),
            pltpu.VMEM((taps * width, channels), bf16),
            pltpu.VMEM((channels, LANES), bf16),
            pltpu.VMEM((n_rows, 8, LANES), bf16),
            pltpu.VMEM((n_rows, width, LANES), bf16),
            pltpu.VMEM((n_rows, 8, LANES), bf16),
            pltpu.VMEM((2, n_rows, 16, channels), bf16),
            pltpu.VMEM((n_rows, width, positions), bf16),
            pltpu.VMEM((9 * width, positions), f32),
            pltpu.VMEM((9 * width, positions), f32),
            pltpu.VMEM((9 * width, positions), f32),
            pltpu.VMEM((width, positions), bf16),
            pltpu.VMEM((width, positions), bf16),
            pltpu.VMEM((width, 4 * positions), bf16),
            pltpu.VMEM((width, 4 * positions), bf16),
            pltpu.VMEM((width, positions), bf16),
            pltpu.VMEM((width, positions), bf16),
            pltpu.VMEM((width, 4 * positions), bf16),
            pltpu.VMEM((width, 4 * positions), bf16),
            pltpu.VMEM((4, n_frames, 1, LANES), f32),
            pltpu.VMEM((4 * n_dp, 1, LANES), f32),
            pltpu.VMEM((4 * n_frames, 4, LANES), f32),
            pltpu.VMEM((n_rows, width, LANES), bf16),
            pltpu.VMEM((n_rows, width, LANES), bf16),
            dma((6,)),
            dma((3,)),
            dma((3,)),
            dma((4,)),
            dma((4,)),
            dma((2,)),
            dma((2,)),
            dma((2, 2)),
            dma((4,)),
            dma((2,)),
            dma((2, 4)),
            pltpu.SemaphoreType.REGULAR((2,)),
        ],
        compiler_params=pltpu.CompilerParams(collective_id=0, has_side_effects=True),
        name="levels",
    )(
        acts_fine.reshape(LANES, channels),
        acts_coarse.reshape(32, channels),
        grad_coarse.reshape(2, 16, channels),
        gain_fine.reshape(1, channels),
        bias_fine.reshape(1, channels),
        gain_coarse.reshape(1, channels),
        bias_coarse.reshape(1, channels),
        kernel_fine.reshape(taps * width, channels),
        kernel_coarse.reshape(taps * width, channels),
    )
    vector = jax.ShapeDtypeStruct((channels // LANES, LANES), f32)
    grad, *vectors = pl.pallas_call(
        finish,
        out_shape=(jax.ShapeDtypeStruct((LANES, channels), bf16), vector, vector, vector, vector),
        in_specs=[vmem, vmem],
        out_specs=(vmem,) * 5,
        name="finish",
    )(*(pltpu.with_memory_space_constraint(x, pltpu.VMEM) for x in (out, par)))
    return (grad.reshape(acts_fine.shape), *(v.reshape(channels) for v in vectors))


def solution(mesh):
    sizes = (mesh.shape["dp"], mesh.shape["frames"], mesh.shape["rows"])
    tall = P("dp", "frames", "rows", None, None)
    in_specs = (tall, tall, tall, P(), P(), P(None, "rows", None), P(), P(), P(None, "rows", None))
    out_specs = (tall, P(), P(), P(), P())
    return jax.shard_map(
        functools.partial(shards, sizes), mesh=mesh, in_specs=in_specs, out_specs=out_specs, check_vma=False
    )
```

```python
import functools

import jax
import jax.numpy as jnp
from jax import lax
from jax.experimental import pallas as pl
from jax.experimental.pallas import tpu as pltpu
from jax.sharding import PartitionSpec as P

GROUPS = 32
EPSILON = 1e-06
MESH = pl.DeviceIdType.MESH
LANES = 128


def iota(shape, dim):
    return lax.broadcasted_iota(jnp.int32, shape, dim)


def one_hot(cond, dtype=jnp.bfloat16):
    return jnp.where(cond, 1.0, 0.0).astype(dtype)


def fine_position(new):
    frame, p, q, a, b = new >> 6, (new >> 5) & 1, (new >> 4) & 1, (new >> 3) & 1, new & 7
    return frame * 64 + (2 * a + p) * 16 + 2 * b + q


def chunk_swap(arrays, chunk):
    arrays = list(arrays)
    for bit in range(3):
        step = 1 << bit
        low = ((chunk >> bit) & 1) == 0
        for i in range(8):
            if i & step:
                continue
            one, two = arrays[i], arrays[i + step]
            arrays[i] = jnp.where(low, one, pltpu.roll(two, 16 * step, 1))
            arrays[i + step] = jnp.where(low, pltpu.roll(one, LANES - 16 * step, 1), two)
    return arrays


def group_total(column):
    per_group = column.shape[0] // 2
    split = column.reshape(2, per_group, 1)
    return jnp.broadcast_to(jnp.sum(split, axis=1, keepdims=True), split.shape).reshape(column.shape)


def row_of(columns, diagonal):
    spread = jnp.zeros(diagonal.shape, jnp.float32)
    for k, column in enumerate(columns):
        spread = jnp.where(diagonal == k, column, spread)
    return jnp.sum(spread, axis=0, keepdims=True)


def column_of(row, diagonal, k):
    return row_sum(jnp.where(diagonal == k, row, 0.0))


def row_sum(x):
    return jnp.sum(x, axis=1, keepdims=True)


def kernel(
    sizes,
    acts_fine_hbm,
    acts_coarse_hbm,
    grad_coarse_hbm,
    gain_fine_hbm,
    bias_fine_hbm,
    gain_coarse_hbm,
    bias_coarse_hbm,
    kernel_fine,
    kernel_coarse,
    out,
    par,
    acts_fine,
    acts_coarse,
    vectors,
    weights_f,
    weights_c,
    sent_f,
    sent_c,
    got_f,
    got_c,
    cot,
    quart,
    prod_0,
    prod_1,
    prod_2,
    halo_out_c,
    halo_in_c,
    halo_out_f,
    halo_in_f,
    here_vals_c,
    prev_vals_c,
    here_vals_f,
    prev_vals_f,
    stats,
    par_z,
    par_xy,
    grad_out,
    grad_in,
    load_sem,
    send_rows,
    recv_rows,
    send_frames,
    recv_frames,
    send_halo,
    recv_halo,
    pass_sem,
    par_sem,
    send_relay,
    recv_relay,
    ready,
):
    n_dp, n_frames, n_rows = sizes
    prods = (prod_0, prod_1, prod_2)
    dp, fr, row = lax.axis_index("dp"), lax.axis_index("frames"), lax.axis_index("rows")
    width = weights_f.shape[0] // 27

    loads = [
        pltpu.make_async_copy(grad_coarse_hbm, cot.at[:, row], load_sem.at[0]),
        pltpu.make_async_copy(acts_coarse_hbm, acts_coarse, load_sem.at[1]),
        pltpu.make_async_copy(acts_fine_hbm, acts_fine, load_sem.at[2]),
        pltpu.make_async_copy(gain_fine_hbm, vectors.at[0], load_sem.at[3]),
        pltpu.make_async_copy(bias_fine_hbm, vectors.at[1], load_sem.at[3]),
        pltpu.make_async_copy(gain_coarse_hbm, vectors.at[2], load_sem.at[3]),
        pltpu.make_async_copy(bias_coarse_hbm, vectors.at[3], load_sem.at[3]),
        pltpu.make_async_copy(kernel_coarse, weights_c, load_sem.at[4]),
        pltpu.make_async_copy(kernel_fine, weights_f, load_sem.at[5]),
    ]
    loads[0].start()

    even = dp + 1 - 2 * lax.rem(dp, 2)
    near_dp = [even] + [lax.rem(core + step, n_dp) for core in (dp, even) for step in (2, n_dp - 2)]
    y, z = lax.div(row, 4), lax.rem(row, 4)
    z_mate = (z, z + 1 - 2 * lax.rem(z, 2), lax.rem(z + 2, 4), 3 - z)
    y_up, y_down, y_far = lax.rem(y + 1, 4), lax.rem(y + 3, 4), lax.rem(y + 2, 4)
    greeted = [{"rows": 4 * y_far + z_of} for z_of in z_mate] + [{"dp": peer} for peer in near_dp]
    greeted += [{"rows": 4 * y_of + z_of} for y_of in (y_up, y_down) for z_of in z_mate]
    greeted += [{"rows": 4 * y + z_of} for z_of in z_mate[1:]]
    greeted += [{"frames": lax.rem(fr + step, n_frames)} for step in range(1, n_frames)]
    barrier = pltpu.get_barrier_semaphore()
    for peer in greeted:
        pl.semaphore_signal(barrier, inc=1, device_id=peer, device_id_type=MESH)

    for load in loads[1:]:
        load.start()

    loads[1].wait()
    place, source = iota((LANES, 32), 0), iota((LANES, 32), 1)
    placed = jnp.dot(one_hot((place & 31) == source), acts_coarse[...], preferred_element_type=jnp.float32)
    quads = placed.T.reshape(n_rows, 4, 8, LANES)
    quad = iota((n_rows, 8, LANES), 2) >> 5
    folded = jnp.where(quad == 0, quads[:, 0], 0.0)
    for k in range(1, 4):
        folded = jnp.where(quad == k, quads[:, k], folded)
    sent_c[...] = folded.astype(jnp.bfloat16)

    loads[0].wait()
    pl.semaphore_wait(barrier, len(greeted))

    def tell(round_):
        for peer in near_dp:
            pl.semaphore_signal(ready.at[round_], inc=1, device_id={"dp": peer}, device_id_type=MESH)

    def told(round_):
        if near_dp:
            pl.semaphore_wait(ready.at[round_], len(near_dp))

    def all_of(ref, sem):
        pltpu.make_async_copy(ref, ref, sem).wait()

    def slices(ref, index):
        return ref.at[pl.ds(pl.multiple_of(index * width, width), width)]

    def rows_copy(stage, target, source):
        if stage == 0:
            src, dst = sent_c.at[target], got_c.at[source]
        elif stage == 1:
            src, dst = slices(sent_f, target), got_f.at[source]
        else:
            src, dst = grad_out.at[target], grad_in.at[source]
        return pltpu.make_async_remote_copy(
            src_ref=src,
            dst_ref=dst,
            send_sem=send_rows.at[stage],
            recv_sem=recv_rows.at[stage],
            device_id={"rows": target},
            device_id_type=MESH,
        )

    def at(y_of, z_of):
        return 4 * y_of + z_of

    def relay(stage, kind, half, slot, target):
        block = cot.at[half, slot] if stage == 0 else quart.at[slot, pl.ds(16 * half, 16)]
        return pltpu.make_async_remote_copy(
            src_ref=block,
            dst_ref=block,
            send_sem=send_relay.at[stage],
            recv_sem=recv_relay.at[stage, kind if kind == last else 2 * kind + half],
            device_id={"rows": target},
            device_id_type=MESH,
        )

    up, down, far = at(y_up, z), at(y_down, z), at(y_far, z)
    last = 6

    def gather_start(stage):
        for kind, target in (
            (0, at(y, z_mate[1])),
            (last, up),
            (last, down),
            (1, at(y, z_mate[2])),
            (2, at(y, z_mate[3])),
            (last, far),
        ):
            for half in range(2):
                relay(stage, kind, half, row, target).start()

    def gather_relay(stage):
        for j in (1, 2, 3):
            slot = at(y, z_mate[j])
            for half in range(2):
                relay(stage, j - 1, half, slot, row).wait_recv()
                for target in (far, up, down):
                    relay(stage, last, half, slot, target).start()

    def gather_finish(stage):
        all_of((cot.at[:, pl.ds(0, 12)], quart.at[pl.ds(0, 12)])[stage], recv_relay.at[stage, last])

    def gather_sent(stage):
        all_of((cot.at[:, pl.ds(0, 15)], quart.at[pl.ds(0, 15)])[stage], send_relay.at[stage])

    def rows_send(stage):
        def step(d, carry):
            rows_copy(stage, lax.rem(row + d, n_rows), row).start()
            return carry

        lax.fori_loop(1, n_rows, step, 0)

    def rows_refs(stage):
        return (got_c, got_f, grad_in)[stage].at[pl.ds(0, n_rows - 1)]

    def rows_wait(stage):
        all_of(rows_refs(stage), recv_rows.at[stage])

    def rows_sent(stage):
        all_of(rows_refs(stage), send_rows.at[stage])

    def frames_copy(stage, target, source):
        return pltpu.make_async_remote_copy(
            src_ref=stats.at[stage, fr],
            dst_ref=stats.at[stage, source],
            send_sem=send_frames.at[stage],
            recv_sem=recv_frames.at[stage],
            device_id={"frames": target},
            device_id_type=MESH,
        )

    def frames_start(stage, block):
        stats[stage, fr] = block

        def step(d, carry):
            frames_copy(stage, lax.rem(fr + d, n_frames), fr).start()
            return carry

        lax.fori_loop(1, n_frames, step, 0)

    def frames_total(stage):
        all_of(stats.at[stage, pl.ds(0, n_frames - 1)], recv_frames.at[stage])
        total = stats[stage, 0]
        for k in range(1, n_frames):
            total = total + stats[stage, k]
        return total

    def halo_copy(stage):
        src, dst = ((halo_out_c, halo_in_c), (halo_out_f, halo_in_f))[stage]
        return pltpu.make_async_remote_copy(
            src_ref=src,
            dst_ref=dst,
            send_sem=send_halo.at[stage],
            recv_sem=recv_halo.at[stage],
            device_id={"frames": lax.rem(fr + n_frames - 1, n_frames)},
            device_id_type=MESH,
        )

    def halo_send(stage):
        @pl.when(fr > 0)
        def _():
            halo_copy(stage).start()

    def halo_wait(stage):
        @pl.when(fr < n_frames - 1)
        def _():
            halo_copy(stage).wait_recv()

        @pl.when(fr == n_frames - 1)
        def _():
            into = (halo_in_c, halo_in_f)[stage]
            into[...] = jnp.zeros_like(into)

    gather_start(0)
    rows_send(0)
    got_c[row] = sent_c[row]
    tell(0)

    loads[2].wait()
    new, old = iota((LANES, LANES), 0), iota((LANES, LANES), 1)
    to_new = one_hot(old == fine_position(new))
    to_old = one_hot(new == fine_position(old))
    moved = jnp.dot(to_new, acts_fine[...], preferred_element_type=jnp.float32)
    sent_f[...] = moved.T.astype(jnp.bfloat16)
    all_of(vectors, load_sem.at[3])

    def pass_on(stage):
        here, there = ((here_vals_c, prev_vals_c), (here_vals_f, prev_vals_f))[stage]
        return pltpu.make_async_remote_copy(
            src_ref=here,
            dst_ref=there,
            send_sem=pass_sem.at[0, stage],
            recv_sem=pass_sem.at[1, stage],
            device_id={"frames": lax.rem(fr + 1, n_frames)},
            device_id_type=MESH,
        )

    def pass_send(stage):
        @pl.when(fr < n_frames - 1)
        def _():
            pass_on(stage).start()

    def pass_wait(stage):
        @pl.when(fr > 0)
        def _():
            pass_on(stage).wait_recv()

        @pl.when(fr == 0)
        def _():
            into = (prev_vals_c, prev_vals_f)[stage]
            into[...] = jnp.zeros_like(into)

    wide = iota((width, vectors.shape[2]), 1) == row * width + iota((width, vectors.shape[2]), 0)

    def column(vector):
        return row_sum(jnp.where(wide, vector, 0.0))

    gain_f, bias_f, gain_c, bias_c = (column(vectors[k]) for k in range(4))
    lane, channel = iota((width, LANES), 1), iota((width, LANES), 0)
    chunk = lane >> 4
    diagonal = jnp.where((lane & 31) == channel, lane >> 5, -1)

    cells = 256
    spot = iota((width, cells), 1)
    top, bottom = spot >= 8, spot < cells - 8
    left, right = (spot & 7) > 0, (spot & 7) < 7

    def above(x):
        return jnp.where(top, pltpu.roll(x, 8, 1), 0.0)

    def below(x):
        return jnp.where(bottom, pltpu.roll(x, cells - 8, 1), 0.0)

    def before(x):
        return jnp.where(left, pltpu.roll(x, 1, 1), 0.0)

    def after(x):
        return jnp.where(right, pltpu.roll(x, cells - 1, 1), 0.0)

    def product(depth, tap, frame):
        return prods[depth][tap * width : (tap + 1) * width, frame * cells : (frame + 1) * cells]

    def spatial_taps(which):
        terms = (((0, 0),), ((1, 0), (0, 1)), ((2, 0), (1, 1)), ((2, 1),))[which]
        taps = []
        for tap in range(9):
            total = product(terms[0][0], tap, terms[0][1])
            for depth, frame in terms[1:]:
                total = total + product(depth, tap, frame)
            taps.append(total)
        return taps

    def coarse_frame(which):
        t = spatial_taps(which)
        r = [below(t[kw]) + t[3 + kw] + above(t[6 + kw]) for kw in range(3)]
        return after(r[0]) + r[1] + before(r[2])

    def fine_frame(which):
        t = spatial_taps(which)
        planes = []
        for p in range(2):
            if p == 0:
                r = [t[kw] + t[3 + kw] + above(t[6 + kw]) for kw in range(3)]
            else:
                r = [below(t[kw]) + t[3 + kw] + t[6 + kw] for kw in range(3)]
            planes.append(r[0] + r[1] + before(r[2]))
            planes.append(after(r[0]) + r[1] + r[2])
        return planes

    gather_relay(0)

    rows_wait(0)
    pieces = [chunk_swap([got_c[8 * half + j].astype(jnp.float32) for j in range(8)], chunk[:8]) for half in range(2)]
    values_c = jnp.concatenate(
        [
            jnp.concatenate([pieces[half][2 * quarter + frame] for quarter in range(4)], axis=0)
            for frame in range(2)
            for half in range(2)
        ],
        axis=1,
    )
    here_vals_c[...] = values_c.astype(jnp.bfloat16)
    frames_start(0, row_of((row_sum(values_c), row_sum(values_c * values_c)), diagonal))
    pass_send(0)
    rows_send(1)
    got_f[row] = sent_f[pl.ds(pl.multiple_of(row * width, width), width), :]

    loads[7].wait()
    told(0)
    tell(1)
    gather_finish(0)
    gathered = cot[...].reshape(2 * n_rows * 16, cot.shape[3])
    nt = (((1,), (1,)), ((), ()))

    def depth_c(depth):
        at = depth * 9 * width
        prods[depth][...] = lax.dot_general(
            weights_c[at : at + 9 * width, :], gathered, nt, preferred_element_type=jnp.float32
        )

    depth_c(0)
    first = coarse_frame(0)
    depth_c(1)
    second = coarse_frame(1)
    conv_before = jnp.concatenate([first, second], axis=1)
    halo_out_c[...] = conv_before.astype(halo_out_c.dtype)
    depth_c(2)
    conv_c = jnp.concatenate([coarse_frame(2), coarse_frame(3)], axis=1)
    picked = one_hot(wide)
    cot_c = lax.dot_general(picked, gathered, nt, preferred_element_type=jnp.float32)

    entries_c = 16 * 2 * n_frames * cells
    entries_f = 4 * entries_c

    def norm_of(moments, entries):
        mean = group_total(column_of(moments, diagonal, 0)) / entries
        square = group_total(column_of(moments, diagonal, 1)) / entries
        return mean, lax.rsqrt(square - mean * mean + EPSILON)

    def through(values, gain, bias, mean, inv):
        normed = (values - mean) * inv
        pre = gain * normed + bias
        squash = jax.nn.sigmoid(pre)
        return normed, squash * (1.0 + pre * (1.0 - squash))

    mean_c, inv_c = norm_of(frames_total(0), entries_c)
    normed_c, slope_c = through(values_c, gain_c, bias_c, mean_c, inv_c)

    def sums_of(conv, normed, slope, conv_before, normed_before, slope_before):
        now, then = conv * slope, conv_before * slope_before
        pairs = ((row_sum(now), row_sum(then)), (row_sum(now * normed), row_sum(then * normed_before)))
        return tuple(own + jnp.where(fr > 0, earlier, 0.0) for own, earlier in pairs)

    pass_wait(0)
    before_c = through(prev_vals_c[...].astype(jnp.float32), gain_c, bias_c, mean_c, inv_c)
    here_c = sums_of(conv_c, normed_c, slope_c, conv_before, *before_c)
    frames_start(1, row_of(here_c, diagonal))
    halo_send(0)

    rows_wait(1)
    swapped = []
    for half in range(2):
        swapped.append(chunk_swap([got_f[8 * half + j].astype(jnp.float32) for j in range(8)], chunk))
    values_f = jnp.concatenate([swapped[half][c] for c in range(8) for half in range(2)], axis=1)
    here_vals_f[...] = values_f.astype(jnp.bfloat16)
    frames_start(2, row_of((row_sum(values_f), row_sum(values_f * values_f)), diagonal))
    pass_send(1)

    halo_wait(0)
    pre_grad_c = (conv_c + halo_in_c[...].astype(jnp.float32)) * slope_c
    base_c, lean_c = cot_c + inv_c * (gain_c * pre_grad_c), inv_c * normed_c
    totals_c = frames_total(1)
    one_c, two_c = column_of(totals_c, diagonal, 0), column_of(totals_c, diagonal, 1)

    def level(base, slope, gain, inv, one, two, entries):
        group_one = group_total(gain * one) / entries
        group_two = group_total(gain * two) / entries
        return base - inv * group_one - slope * group_two

    level_c = level(base_c, lean_c, gain_c, inv_c, one_c, two_c, entries_c)
    quarter = (level_c * 0.25).astype(jnp.bfloat16)
    quart[row] = quarter
    gather_start(1)
    gather_relay(1)
    mean_f, inv_f = norm_of(frames_total(2), entries_f)
    normed_f, slope_f = through(here_vals_f[...].astype(jnp.float32), gain_f, bias_f, mean_f, inv_f)
    pass_wait(1)
    before_f = through(prev_vals_f[...].astype(jnp.float32), gain_f, bias_f, mean_f, inv_f)
    gather_finish(1)

    loads[8].wait()
    quarters = quart[...].reshape(n_rows * width, 2 * cells)

    def depth_f(depth):
        at = depth * 9 * width
        prods[depth][...] = jnp.dot(
            weights_f[at : at + 9 * width, :], quarters, preferred_element_type=jnp.float32
        )

    depth_f(0)
    first = fine_frame(0)
    depth_f(1)
    second = fine_frame(1)
    conv_before = jnp.concatenate(first + second, axis=1)
    halo_out_f[...] = conv_before.astype(halo_out_f.dtype)
    halo_send(1)
    depth_f(2)
    conv_f = jnp.concatenate(fine_frame(2) + fine_frame(3), axis=1)
    here_f = sums_of(conv_f, normed_f, slope_f, conv_before, *before_f)

    cells_all = n_dp * 2 * n_frames * cells
    scale_c, scale_f = 1.0 / cells_all**0.5, 1.0 / (4 * cells_all) ** 0.5
    n_z, n_xy = 4 * n_dp, 4 * n_frames
    in_z, in_xy = 4 * dp + z, 4 * fr + y

    def z_copy(dp_of, z_of):
        return pltpu.make_async_remote_copy(
            src_ref=par_z.at[in_z],
            dst_ref=par_z.at[in_z],
            send_sem=par_sem.at[0],
            recv_sem=par_sem.at[1],
            device_id={"dp": dp_of, "rows": 4 * y + z_of},
            device_id_type=MESH,
        )

    def xy_copy(fr_of, y_of):
        return pltpu.make_async_remote_copy(
            src_ref=par_xy.at[in_xy],
            dst_ref=par_xy.at[in_xy],
            send_sem=par_sem.at[2],
            recv_sem=par_sem.at[3],
            device_id={"frames": fr_of, "rows": 4 * y_of + z},
            device_id_type=MESH,
        )

    mine = (here_f[1] * scale_f, here_f[0] * scale_f, here_c[1] * scale_c, here_c[0] * scale_c)
    par_z[in_z] = row_of(mine, diagonal)
    told(1)
    for step in (4, 5, 3, 6, 2, 7, 1):
        there = lax.rem(dp + step, n_dp)
        for k in range(4):
            z_copy(there, k).start()
    for k in (1, 2, 3):
        z_copy(dp, z_mate[k]).start()
    frames_start(3, row_of(here_f, diagonal))
    halo_wait(1)
    pre_grad_f = (conv_f + halo_in_f[...].astype(jnp.float32)) * slope_f
    four = [quarter[:, frame * cells : (frame + 1) * cells].astype(jnp.float32) for frame in range(2)]
    cot_f = jnp.concatenate([four[c // 4] for c in range(8)], axis=1)
    base_f, lean_f = cot_f + inv_f * (gain_f * pre_grad_f), inv_f * normed_f
    totals_f = frames_total(3)
    one_f, two_f = column_of(totals_f, diagonal, 0), column_of(totals_f, diagonal, 1)

    level_f = level(base_f, lean_f, gain_f, inv_f, one_f, two_f, entries_f)
    for half in range(2):
        planes = [level_f[:, c * cells + half * LANES : c * cells + (half + 1) * LANES] for c in range(8)]
        for j, block in enumerate(chunk_swap(planes, chunk)):
            grad_out[8 * half + j] = block.astype(jnp.bfloat16)
    rows_send(2)
    grad_in[row] = grad_out[row]

    gather_sent(0)
    gather_sent(1)
    for stage in range(2):
        rows_sent(stage)
    for stage in range(4):
        all_of(stats.at[stage, pl.ds(0, n_frames - 1)], send_frames.at[stage])

    @pl.when(fr > 0)
    def _():
        halo_copy(0).wait_send()
        halo_copy(1).wait_send()

    @pl.when(fr < n_frames - 1)
    def _():
        pass_on(0).wait_send()
        pass_on(1).wait_send()

    all_of(par_z.at[pl.ds(0, n_z - 1)], par_sem.at[1])
    for k in range(4):
        total = par_z[k]
        for j in range(1, n_dp):
            total = total + par_z[4 * j + k]
        par_xy[in_xy, k : k + 1] = total
    for step in (2, 1, 3):
        there = lax.rem(fr + step, n_frames)
        for k in range(4):
            xy_copy(there, k).start()
    for k in (y_far, y_up, y_down):
        xy_copy(fr, k).start()

    rows_wait(2)
    back = grad_in[...].reshape(n_rows * width, LANES).astype(jnp.float32).T.astype(jnp.bfloat16)
    out[...] = jnp.dot(to_old, back, preferred_element_type=jnp.float32).astype(out.dtype)

    rows_sent(2)
    all_of(par_z.at[pl.ds(0, n_z - 1)], par_sem.at[0])
    all_of(par_xy.at[pl.ds(0, n_xy - 1)], par_sem.at[3])
    sums = []
    for k in range(4):
        total = par_xy[k]
        for j in range(1, n_frames):
            total = total + par_xy[4 * j + k]
        sums.append(total)
    lines = [jnp.concatenate([sums[k][j : j + 1] for k in range(4)], axis=0) for j in range(4)]
    part = iota(lines[0].shape, 1) >> 5
    for bit in range(2):
        step = 1 << bit
        low = ((part >> bit) & 1) == 0
        for i in range(4):
            if i & step:
                continue
            one, two = lines[i], lines[i + step]
            lines[i] = jnp.where(low, one, pltpu.roll(two, 32 * step, 1))
            lines[i + step] = jnp.where(low, pltpu.roll(one, LANES - 32 * step, 1), two)
    for k in range(4):
        par[k] = lines[k]

    all_of(par_xy.at[pl.ds(0, n_xy - 1)], par_sem.at[2])


def finish(grad, par, out, *vectors):
    out[...] = grad[...]
    for k, vector in enumerate(vectors):
        vector[...] = par[k]


def shards(
    sizes,
    acts_fine,
    acts_coarse,
    grad_coarse,
    gain_fine,
    bias_fine,
    kernel_fine,
    gain_coarse,
    bias_coarse,
    kernel_coarse,
):
    n_dp, n_frames, n_rows = sizes
    channels = acts_fine.shape[-1]
    width = channels // n_rows
    positions = 2 * n_rows * 16
    bf16, f32 = jnp.bfloat16, jnp.float32
    vmem = pl.BlockSpec(memory_space=pltpu.VMEM)
    anywhere = pl.BlockSpec(memory_space=pl.ANY)
    dma = pltpu.SemaphoreType.DMA
    taps = kernel_fine.shape[0]
    held = (pltpu.VMEM((LANES, channels), bf16), pltpu.VMEM((4, channels // LANES, LANES), f32))
    out, par = pl.pallas_call(
        functools.partial(kernel, sizes),
        out_shape=held,
        in_specs=[anywhere] * 9,
        out_specs=(vmem, vmem),
        scratch_shapes=[
            pltpu.VMEM((LANES, channels), bf16),
            pltpu.VMEM((32, channels), bf16),
            pltpu.VMEM((4, 1, channels), f32),
            pltpu.VMEM((taps * width, channels), bf16),
            pltpu.VMEM((taps * width, channels), bf16),
            pltpu.VMEM((channels, LANES), bf16),
            pltpu.VMEM((n_rows, 8, LANES), bf16),
            pltpu.VMEM((n_rows, width, LANES), bf16),
            pltpu.VMEM((n_rows, 8, LANES), bf16),
            pltpu.VMEM((2, n_rows, 16, channels), bf16),
            pltpu.VMEM((n_rows, width, positions), bf16),
            pltpu.VMEM((9 * width, positions), f32),
            pltpu.VMEM((9 * width, positions), f32),
            pltpu.VMEM((9 * width, positions), f32),
            pltpu.VMEM((width, positions), bf16),
            pltpu.VMEM((width, positions), bf16),
            pltpu.VMEM((width, 4 * positions), bf16),
            pltpu.VMEM((width, 4 * positions), bf16),
            pltpu.VMEM((width, positions), bf16),
            pltpu.VMEM((width, positions), bf16),
            pltpu.VMEM((width, 4 * positions), bf16),
            pltpu.VMEM((width, 4 * positions), bf16),
            pltpu.VMEM((4, n_frames, 1, LANES), f32),
            pltpu.VMEM((4 * n_dp, 1, LANES), f32),
            pltpu.VMEM((4 * n_frames, 4, LANES), f32),
            pltpu.VMEM((n_rows, width, LANES), bf16),
            pltpu.VMEM((n_rows, width, LANES), bf16),
            dma((6,)),
            dma((3,)),
            dma((3,)),
            dma((4,)),
            dma((4,)),
            dma((2,)),
            dma((2,)),
            dma((2, 2)),
            dma((4,)),
            dma((2,)),
            dma((2, 7)),
            pltpu.SemaphoreType.REGULAR((2,)),
        ],
        compiler_params=pltpu.CompilerParams(collective_id=0, has_side_effects=True),
        name="levels",
    )(
        acts_fine.reshape(LANES, channels),
        acts_coarse.reshape(32, channels),
        grad_coarse.reshape(2, 16, channels),
        gain_fine.reshape(1, channels),
        bias_fine.reshape(1, channels),
        gain_coarse.reshape(1, channels),
        bias_coarse.reshape(1, channels),
        kernel_fine.reshape(taps * width, channels),
        kernel_coarse.reshape(taps * width, channels),
    )
    vector = jax.ShapeDtypeStruct((channels // LANES, LANES), f32)
    grad, *vectors = pl.pallas_call(
        finish,
        out_shape=(jax.ShapeDtypeStruct((LANES, channels), bf16), vector, vector, vector, vector),
        in_specs=[vmem, vmem],
        out_specs=(vmem,) * 5,
        name="finish",
    )(*(pltpu.with_memory_space_constraint(x, pltpu.VMEM) for x in (out, par)))
    return (grad.reshape(acts_fine.shape), *(v.reshape(channels) for v in vectors))


def solution(mesh):
    sizes = (mesh.shape["dp"], mesh.shape["frames"], mesh.shape["rows"])
    tall = P("dp", "frames", "rows", None, None)
    in_specs = (tall, tall, tall, P(), P(), P(None, "rows", None), P(), P(), P(None, "rows", None))
    out_specs = (tall, P(), P(), P(), P())
    return jax.shard_map(
        functools.partial(shards, sizes), mesh=mesh, in_specs=in_specs, out_specs=out_specs, check_vma=False
    )
```
